32 devices in a mesh: site: 4 (over y, x), sector: 8 (over z, core).
Axes of the slice: x: 2, y: 2, z: 4, core: 2. Of those that a mesh axis runs over, the one named last changes fastest.
Arguments:
- env_in: bfloat16 [2, 8, 512, 512], P(None, 'sector'), may hold values from -6 to 6
- bra: bfloat16 [4, 4, 8, 512, 512], P('site', None, 'sector'), may hold values from -0.25 to 0.25
- ket: bfloat16 [4, 2, 4, 8, 512, 512], P('site', None, None, 'sector'), may hold values from -0.125 to 0.125
- sector_dims: int32 [5, 8], replicated, may hold values from 384 to 512, as said below
- flags: int32 [4, 4, 8], P('site', None, 'sector'), may hold values 0 or 1
Outputs:
- env_after: bfloat16 [4, 2, 8, 512, 512], P('site', None, 'sector')
The draws below stay inside these ranges and needn't reach their ends.
Inputs may be any that keep to these rules, and one draw needn't show every extreme that they name: `sector_dims`: every bond has some sector whose used size is exactly 512.
All inputs are finite; a program needn't handle non-finite values. No bound on the sum of `flags` on one device may be relied on, other than what follows from the above.
Results may differ from the reference program's by a relative error of at most 0.013.
Values may be sent and summed in bfloat16 or wider, within the bound.
No kernel may reach another device: no remote copies, remote signals or barrier semaphores. Data moves between devices by JAX's collectives and lax.ppermute only.
A program may use at most 64 MiB of HBM per device.

```python
import jax
import jax.numpy as jnp

P_SIZE = 512
PAIRS = 2
SECTORS = 8
N_SITE = 4


def draw_sector_dims(key, part):
    first_key = jax.random.fold_in(key, 11)
    second_key = jax.random.fold_in(key, 23)
    lowest = 3 * P_SIZE // 4
    dims = jax.random.randint(first_key, (N_SITE + 1, SECTORS), lowest, P_SIZE + 1)
    placed = jax.random.randint(second_key, (N_SITE + 1,), 0, SECTORS)
    column = jnp.arange(SECTORS)[None, :]
    dims = jnp.where(column == placed[:, None], P_SIZE, dims)
    return dims.astype(jnp.int32)


def touch_ends(array, key, low, largest):
    place = [jax.random.randint(jax.random.fold_in(key, axis), (), 0, length) for axis, length in enumerate(array.shape)]
    widest = array.shape.index(max(array.shape))
    beside = place[:widest] + [(place[widest] + 1) % array.shape[widest]] + place[widest + 1:]
    return array.at[tuple(place)].set(low).at[tuple(beside)].set(largest)


def shard_levels(rng, shape, pieces, low, high):
    loudness = 1.0
    for dim, shards_of in pieces:
        steps = jax.random.uniform(jax.random.fold_in(jax.random.fold_in(rng, 6), dim), (shards_of,), jnp.float32, low / len(pieces), high / len(pieces))
        loudness = loudness * jnp.repeat(jnp.exp(steps), shape[dim] // shards_of).reshape((-1,) + (1,) * (len(shape) - 1 - dim))
    return loudness


def normal_values(rng, shape, deviation, most, pieces=(), dtype=jnp.bfloat16):
    result = jax.random.normal(rng, shape, jnp.float32) * deviation
    if len(pieces) > 0:
        result = shard_levels(rng, shape, pieces, -0.22, 0.18) * result
    return jnp.clip(result, min=-most, max=most).astype(dtype)


def setup_inputs(seed: int = 0) -> dict:
    streams_of = jax.random.split(jax.random.key(seed), 6)
    return {
        "env_in": normal_values(streams_of[0], (PAIRS, SECTORS, P_SIZE, P_SIZE), 1.0, 6.0, ((1, 8),)),
        "bra": normal_values(streams_of[1], (N_SITE, 4, SECTORS, P_SIZE, P_SIZE), P_SIZE ** -0.5, 0.25, ((0, 4), (2, 8))),
        "ket": normal_values(streams_of[2], (N_SITE, PAIRS, 4, SECTORS, P_SIZE, P_SIZE), (4 * P_SIZE) ** -0.5, 0.125, ((0, 4), (3, 8))),
        "sector_dims": draw_sector_dims(jax.random.fold_in(streams_of[5], 71), 0),
        "flags": touch_ends((jax.random.randint(streams_of[4], (N_SITE, 4, SECTORS), 0, 4) < 3).astype(jnp.int32), jax.random.fold_in(streams_of[4], 1), 0, 1),
    }


def window_mask(sector_dims, bond):
    lanes = jnp.arange(P_SIZE)
    keep = (lanes[None, :] < sector_dims[bond][:, None]).astype(jnp.float32)
    return keep[:, :, None] * keep[:, None, :]


def raise_charge(blocks, amount):
    zeros = jnp.zeros((amount, P_SIZE, P_SIZE), jnp.float32)
    return jnp.concatenate([zeros, blocks[:-amount]], axis=0)


def reference(env_in, bra, ket, sector_dims, flags):
    first = window_mask(sector_dims, 0)
    envs = [(env_in[p].astype(jnp.float32) * first).astype(jnp.bfloat16) for p in range(PAIRS)]
    results = []
    for site_now in range(N_SITE):
        window = window_mask(sector_dims, site_now + 1)
        weights = flags[site_now].astype(jnp.float32)[:, :, None, None]
        layer = []
        for pair in range(PAIRS):
            moved = jnp.einsum("qab,sqbc->sqac", envs[pair].astype(jnp.float32), ket[site_now, pair].astype(jnp.float32)).astype(jnp.bfloat16)
            partial_value = jnp.einsum("sqba,sqbc->sqac", bra[site_now].astype(jnp.float32), moved.astype(jnp.float32)) * weights
            total = partial_value[0] + raise_charge(partial_value[1] + partial_value[2], 1) + raise_charge(partial_value[3], 2)
            fresh = (total * window).astype(jnp.bfloat16)
            layer.append(fresh)
            envs[pair] = fresh
        results.append(jnp.stack(layer, axis=0))
    return jnp.stack(results, axis=0)
```

```python
import functools

import jax
import jax.numpy as jnp
from jax import lax
from jax.experimental import pallas as pl
from jax.experimental.pallas import tpu as pltpu
from jax.sharding import PartitionSpec as P

CHUNKS = 2
AXES = ("site", "sector")
LIMIT = 20 << 20
SMEM = pl.BlockSpec(memory_space=pltpu.SMEM)
VMEM = pl.BlockSpec(memory_space=pltpu.VMEM)
ANY = pl.BlockSpec(memory_space=pl.ANY)


def bounds(width):
    tile = 16
    return [width * k // CHUNKS // tile * tile for k in range(CHUNKS + 1)]


def across(a, b):
    return lax.dot_general(a, b, (((1,), (0,)), ((), ())), preferred_element_type=jnp.float32)


def down(a, b):
    return lax.dot_general(a, b, (((0,), (0,)), ((), ())), preferred_element_type=jnp.float32)


def inside(shape, row, used):
    rows = lax.broadcasted_iota(jnp.int32, shape, 0) + row
    lanes = lax.broadcasted_iota(jnp.int32, shape, 1)
    return jnp.logical_and(rows < used, lanes < used)


def pair_of(step, pairs):
    return jnp.clip(step - lax.axis_index("site"), 0, pairs - 1)


def cut(block, row, dims):
    used = dims[0, lax.axis_index("sector")]
    return jnp.where(inside(block.shape, row, used), block.astype(jnp.float32), 0.0).astype(jnp.bfloat16)


def product(e, ket_block, bra_rows, flag):
    moved = across(e, ket_block) * flag.astype(jnp.float32)
    return down(bra_rows, moved.astype(jnp.bfloat16))


def group(states, e, row, ket, bra, flags, pair, total):
    rows = slice(row, row + e.shape[0])
    for s in states:
        part = product(e, ket[0, pair, s, 0], bra[0, s, 0, rows], flags[0, s, 0])
        total = part if total is None else total + part
    return total


def open_kernel(step, groups, dims, flags, env, ket, bra, *refs):
    outs = refs[: len(groups)]
    env_buf, ket_buf, bra_buf, sems = refs[len(groups) :]
    pairs = ket.shape[1]
    states = [s for states in groups for s in states]
    pair = pair_of(step, pairs)
    first = pltpu.make_async_copy(env.at[step, 0], env_buf, sems.at[0])
    first.start()
    copies = []
    for i, s in enumerate(states):
        copies.append(
            (
                pltpu.make_async_copy(ket.at[0, pair, s, 0], ket_buf.at[i], sems.at[1 + 2 * i]),
                pltpu.make_async_copy(bra.at[0, s, 0], bra_buf.at[i], sems.at[2 + 2 * i]),
            )
        )
        for copy in copies[-1]:
            copy.start()
    first.wait()
    e = cut(env_buf[...], 0, dims)
    i = 0
    for states, out in zip(groups, outs):
        total = None
        for s in states:
            for copy in copies[i]:
                copy.wait()
            part = product(e, ket_buf[i], bra_buf[i], flags[0, s, 0])
            total = part if total is None else total + part
            i += 1
        out[...] = total.astype(jnp.bfloat16)


def step_kernel(step, row, fresh, added, groups, dims, flags, *refs):
    refs = list(refs)
    env = refs.pop(0) if fresh else None
    held, ket, bra = refs[:3]
    before = refs[3 : 3 + len(groups)] if added else [None] * len(groups)
    outs = refs[3 + len(groups) * added :]
    pair = pair_of(step, ket.shape[1])
    e = held[...]
    if fresh:
        entering = cut(env[step, 0, row : row + e.shape[0]], row, dims)
        e = jnp.where(lax.axis_index("site") == 0, entering, e)
    for states, start, out in zip(groups, before, outs):
        total = group(states, e, row, ket, bra, flags, pair, None if start is None else start[...])
        out[...] = total.astype(out.dtype)


def sum_kernel(row, bond_site, dims, none, other, came, out):
    rows = slice(row, row + came.shape[0])
    sector = lax.axis_index("sector")
    used = dims[lax.axis_index("site") + 1, sector]
    total = none[rows].astype(jnp.float32)
    total = total + jnp.where(sector % 2 == 1, other[rows].astype(jnp.float32), 0.0)
    total = total + jnp.where(sector >= 2, came[...].astype(jnp.float32), 0.0)
    out[...] = jnp.where(inside(total.shape, row, used), total, 0.0).astype(jnp.bfloat16)


def write_kernel(step, cuts, pairs, *refs):
    blocks = refs[: len(cuts) - 1]
    out, sems = refs[-2:]
    pair = step - lax.axis_index("site")

    @pl.when(jnp.logical_and(pair >= 0, pair < pairs))
    def _():
        copies = []
        for k, block in enumerate(blocks):
            rows = pl.ds(cuts[k], cuts[k + 1] - cuts[k])
            copies.append(pltpu.make_async_copy(block, out.at[0, pair, 0, rows], sems.at[k]))
            copies[-1].start()
        for copy in copies:
            copy.wait()


def call(kernel, in_specs, out_shape, flops=0, moved=0, **more):
    return pl.pallas_call(
        kernel,
        out_shape=out_shape,
        in_specs=in_specs,
        compiler_params=pltpu.CompilerParams(vmem_limit_bytes=LIMIT),
        cost_estimate=pl.CostEstimate(flops=flops, bytes_accessed=moved, transcendentals=0),
        **more,
    )


def per_device(env_in, bra, ket, sector_dims, flags):
    sections = lax.axis_size("site")
    sectors = lax.axis_size("sector")
    sector = lax.axis_index("sector")
    pairs = ket.shape[1]
    width = ket.shape[-1]
    steps = pairs + sections - 1
    cuts = bounds(width)
    even = sector % 2 == 0

    def at(j, q):
        return j * sectors + q

    everyone = [(j, q) for j in range(sections) for q in range(sectors)]
    swap_pairs = [(at(j, q), at(j, q ^ 1)) for j, q in everyone]
    up_pairs = [(at(j, q), at(j, (q + 2) % sectors)) for j, q in everyone]
    next_pairs = [(at(j, q), at((j + 1) % sections, q)) for j, q in everyone]

    def block(rows, dtype=jnp.bfloat16):
        return jax.ShapeDtypeStruct((rows, width), dtype)

    def opening(groups):
        count = sum(len(states) for states in groups)
        scratch = [
            pltpu.VMEM((width, width), jnp.bfloat16),
            pltpu.VMEM((count, width, width), jnp.bfloat16),
            pltpu.VMEM((count, width, width), jnp.bfloat16),
            pltpu.SemaphoreType.DMA((1 + 2 * count,)),
        ]
        return call(
            functools.partial(open_kernel, 0, groups),
            [SMEM, SMEM, ANY, ANY, ANY],
            [block(width)] * len(groups),
            4 * count * width**3,
            scratch_shapes=scratch,
            out_specs=[VMEM] * len(groups),
        )(sector_dims, flags, env_in, ket, bra)

    def chunk(step, k, groups, held, before, dtype):
        fresh = step < pairs
        operands = [sector_dims, flags] + ([env_in] if fresh else []) + [held, ket, bra] + before
        return call(
            functools.partial(step_kernel, step, cuts[k], fresh, len(before) > 0, groups),
            [SMEM, SMEM] + [VMEM] * (len(operands) - 2),
            [block(width, dtype)] * len(groups),
            4 * sum(len(states) for states in groups) * (cuts[k + 1] - cuts[k]) * width**2,
            out_specs=[VMEM] * len(groups),
        )(*operands)

    result = None
    held = None
    for step in range(steps):
        if step == 0:
            (single,) = opening([(1, 2)])
            other = lax.ppermute(single, AXES, swap_pairs)
            double, none = opening([(3,), (0,)])
        else:
            total = []
            for k in range(CHUNKS - 1):
                total = chunk(step, k, [(1, 2), (3,), (0,)], held[k], list(total), jnp.float32)
            total = list(total)
            (single,) = chunk(step, CHUNKS - 1, [(1, 2)], held[-1], total[:1], jnp.bfloat16)
            other = lax.ppermute(single, AXES, swap_pairs)
            double, none = chunk(step, CHUNKS - 1, [(3,), (0,)], held[-1], total[1:], jnp.bfloat16)
        fresh = []
        for k in range(CHUNKS):
            rows = slice(cuts[k], cuts[k + 1])
            part = jnp.where(even, other[rows].astype(jnp.float32), 0.0)
            up = (double[rows].astype(jnp.float32) + part).astype(jnp.bfloat16)
            came = lax.ppermute(up, AXES, up_pairs)
            fresh.append(
                call(
                    functools.partial(sum_kernel, cuts[k], step),
                    [SMEM] + [VMEM] * 3,
                    block(cuts[k + 1] - cuts[k]),
                    out_specs=VMEM,
                )(sector_dims, none, other, came)
            )
        if step + 1 < steps:
            held = [lax.ppermute(rows, AXES, next_pairs) for rows in fresh]
        shape = jax.ShapeDtypeStruct((1, pairs, 1, width, width), jnp.bfloat16)
        operands = fresh + ([] if result is None else [result])
        result = call(
            functools.partial(write_kernel, step, cuts, pairs),
            [VMEM] * CHUNKS + [ANY] * (len(operands) - CHUNKS),
            shape,
            out_specs=ANY,
            scratch_shapes=[pltpu.SemaphoreType.DMA((CHUNKS,))],
            input_output_aliases={} if result is None else {CHUNKS: 0},
        )(*operands)
    return result


def solution(mesh):
    in_specs = (
        P(None, "sector", None, None),
        P("site", None, "sector", None, None),
        P("site", None, None, "sector", None, None),
        P(),
        P("site", None, "sector"),
    )
    out_specs = P("site", None, "sector", None, None)
    return jax.shard_map(per_device, mesh=mesh, in_specs=in_specs, out_specs=out_specs, check_vma=False)
```

```python
import functools

import jax
import jax.numpy as jnp
from jax import lax
from jax.experimental import pallas as pl
from jax.experimental.pallas import tpu as pltpu
from jax.sharding import PartitionSpec as P

CHUNKS = 3
AXES = ("site", "sector")
LIMIT = 20 << 20
OPEN_LIMIT = 60 << 20
SMEM = pl.BlockSpec(memory_space=pltpu.SMEM)
VMEM = pl.BlockSpec(memory_space=pltpu.VMEM)
ANY = pl.BlockSpec(memory_space=pl.ANY)


def bounds(width):
    tile = 16
    return [width * k // CHUNKS // tile * tile for k in range(CHUNKS + 1)]


def across(a, b):
    return lax.dot_general(a, b, (((1,), (0,)), ((), ())), preferred_element_type=jnp.float32)


def down(a, b):
    return lax.dot_general(a, b, (((0,), (0,)), ((), ())), preferred_element_type=jnp.float32)


def inside(shape, row, used):
    rows = lax.broadcasted_iota(jnp.int32, shape, 0) + row
    lanes = lax.broadcasted_iota(jnp.int32, shape, 1)
    return jnp.logical_and(rows < used, lanes < used)


def pair_of(step, pairs):
    return jnp.clip(step - lax.axis_index("site"), 0, pairs - 1)


def cut(block, row, dims):
    used = dims[0, lax.axis_index("sector")]
    return jnp.where(inside(block.shape, row, used), block.astype(jnp.float32), 0.0).astype(jnp.bfloat16)


def product(e, ket_block, bra_rows, flag):
    moved = across(e, ket_block) * flag
    return down(bra_rows, moved.astype(jnp.bfloat16))


def group(states, e, row, ket, bra, flags, pair, total):
    rows = slice(row, row + e.shape[0])
    for s in states:
        part = product(e, ket[0, pair, s, 0], bra[0, s, 0, rows], flags[s, :1])
        total = part if total is None else total + part
    return total


def open_kernel(step, groups, dims, flags, env, ket, bra, *refs):
    outs = refs[: len(groups)]
    env_buf, ket_buf, bra_buf, sems = refs[len(groups) :]
    pairs = ket.shape[1]
    states = [s for states in groups for s in states]
    pair = pair_of(step, pairs)
    first = pltpu.make_async_copy(env.at[step, 0], env_buf, sems.at[0])
    first.start()
    copies = []
    for i, s in enumerate(states):
        copies.append(
            (
                pltpu.make_async_copy(ket.at[0, pair, s, 0], ket_buf.at[i], sems.at[1 + 2 * i]),
                pltpu.make_async_copy(bra.at[0, s, 0], bra_buf.at[i], sems.at[2 + 2 * i]),
            )
        )
        for copy in copies[-1]:
            copy.start()
    first.wait()
    e = cut(env_buf[...], 0, dims)
    i = 0
    for states, out in zip(groups, outs):
        total = None
        for s in states:
            for copy in copies[i]:
                copy.wait()
            part = product(e, ket_buf[i], bra_buf[i], flags[0, s, 0].astype(jnp.float32))
            total = part if total is None else total + part
            i += 1
        out[...] = total.astype(jnp.bfloat16)


def setup_kernel(dims, flags, env, after, window, flag_rows, entering):
    del after
    used = dims[lax.axis_index("site") + 1, lax.axis_index("sector")]
    window[...] = jnp.where(inside(window.shape, 0, used), 1.0, 0.0).astype(window.dtype)
    for s in range(flag_rows.shape[0]):
        flag_rows[s] = jnp.zeros(flag_rows.shape[1:], jnp.float32) + flags[0, s, 0].astype(jnp.float32)
    for p in range(entering.shape[0]):
        entering[p] = cut(env[p + 1, 0], 0, dims)


def step_kernel(step, row, fresh, added, groups, flags, *refs):
    refs = list(refs)
    entering = refs.pop(0) if fresh else None
    held, ket, bra = refs[:3]
    before = refs[3 : 3 + len(groups)] if added else [None] * len(groups)
    outs = refs[3 + len(groups) * added :]
    pair = pair_of(step, ket.shape[1])
    e = held[...]
    if fresh:
        e = jnp.where(lax.axis_index("site") == 0, entering[step - 1, row : row + e.shape[0]], e)
    for states, start, out in zip(groups, before, outs):
        total = group(states, e, row, ket, bra, flags, pair, None if start is None else start[...])
        out[...] = total.astype(out.dtype)


def summed(row, window, none, other, came):
    rows = slice(row, row + came.shape[0])
    sector = lax.axis_index("sector")
    total = none[rows].astype(jnp.float32)
    total = total + jnp.where(sector % 2 == 1, other[rows].astype(jnp.float32), 0.0)
    total = total + jnp.where(sector >= 2, came[...].astype(jnp.float32), 0.0)
    return (total * window[rows].astype(jnp.float32)).astype(jnp.bfloat16)


def sum_kernel(row, window, none, other, came, out):
    out[...] = summed(row, window, none, other, came)


def written(pair, pairs, row, block, out, sem):
    @pl.when(jnp.logical_and(pair >= 0, pair < pairs))
    def _():
        copy = pltpu.make_async_copy(block, out.at[0, pair, 0, pl.ds(row, block.shape[0])], sem)
        copy.start()
        copy.wait()


def write_kernel(step, cuts, pairs, *refs):
    blocks = refs[: len(cuts) - 1]
    out, sems = refs[-2:]
    pair = step - lax.axis_index("site")

    @pl.when(jnp.logical_and(pair >= 0, pair < pairs))
    def _():
        copies = []
        for k, block in enumerate(blocks):
            rows = pl.ds(cuts[k], cuts[k + 1] - cuts[k])
            copies.append(pltpu.make_async_copy(block, out.at[0, pair, 0, rows], sems.at[k]))
            copies[-1].start()
        for copy in copies:
            copy.wait()


def last_kernel(step, pairs, row, window, none, other, came, before, out, block, sem):
    del before
    block[...] = summed(row, window, none, other, came)
    written(step - lax.axis_index("site"), pairs, row, block, out, sem)


def call(kernel, in_specs, out_shape, flops=0, moved=0, limit=LIMIT, **more):
    return pl.pallas_call(
        kernel,
        out_shape=out_shape,
        in_specs=in_specs,
        compiler_params=pltpu.CompilerParams(vmem_limit_bytes=limit),
        cost_estimate=pl.CostEstimate(flops=flops, bytes_accessed=moved, transcendentals=0),
        **more,
    )


def per_device(env_in, bra, ket, sector_dims, flags):
    sections = lax.axis_size("site")
    sectors = lax.axis_size("sector")
    sector = lax.axis_index("sector")
    pairs = ket.shape[1]
    width = ket.shape[-1]
    steps = pairs + sections - 1
    cuts = bounds(width)
    even = sector % 2 == 0

    def at(j, q):
        return j * sectors + q

    everyone = [(j, q) for j in range(sections) for q in range(sectors)]
    swap_pairs = [(at(j, q), at(j, q ^ 1)) for j, q in everyone]
    up_pairs = [(at(j, q), at(j, (q + 2) % sectors)) for j, q in everyone]
    next_pairs = [(at(j, q), at((j + 1) % sections, q)) for j, q in everyone]

    def block(rows, dtype=jnp.bfloat16):
        return jax.ShapeDtypeStruct((rows, width), dtype)

    def opening(groups):
        count = sum(len(states) for states in groups)
        scratch = [
            pltpu.VMEM((width, width), jnp.bfloat16),
            pltpu.VMEM((count, width, width), jnp.bfloat16),
            pltpu.VMEM((count, width, width), jnp.bfloat16),
            pltpu.SemaphoreType.DMA((1 + 2 * count,)),
        ]
        return call(
            functools.partial(open_kernel, 0, groups),
            [SMEM, SMEM, ANY, ANY, ANY],
            [block(width)] * len(groups),
            4 * count * width**3,
            limit=OPEN_LIMIT,
            scratch_shapes=scratch,
            out_specs=[VMEM] * len(groups),
        )(sector_dims, flags, env_in, ket, bra)

    def chunk(step, k, groups, held, before, dtype):
        fresh = step < pairs
        operands = [flag_rows] + ([entering] if fresh else []) + [held, ket, bra] + before
        return call(
            functools.partial(step_kernel, step, cuts[k], fresh, len(before) > 0, groups),
            [VMEM] * len(operands),
            [block(width, dtype)] * len(groups),
            4 * sum(len(states) for states in groups) * (cuts[k + 1] - cuts[k]) * width**2,
            out_specs=[VMEM] * len(groups),
        )(*operands)

    whole = jax.ShapeDtypeStruct((1, pairs, 1, width, width), jnp.bfloat16)
    result = None
    held = None
    for step in range(steps):
        if step == 0:
            (single,) = opening([(1, 2)])
            other = lax.ppermute(single, AXES, swap_pairs)
            double, none = opening([(3,), (0,)])
            window, flag_rows, entering = call(
                setup_kernel,
                [SMEM, SMEM, VMEM, ANY],
                [
                    block(width),
                    jax.ShapeDtypeStruct((ket.shape[2], 8, width), jnp.float32),
                    jax.ShapeDtypeStruct((max(pairs - 1, 1), width, width), jnp.bfloat16),
                ],
                out_specs=[VMEM] * 3,
            )(sector_dims, flags, env_in, double)
        else:
            total = []
            for k in range(CHUNKS - 1):
                total = chunk(step, k, [(1, 2), (3,), (0,)], held[k], list(total), jnp.float32)
            total = list(total)
            (single,) = chunk(step, CHUNKS - 1, [(1, 2)], held[-1], total[:1], jnp.bfloat16)
            other = lax.ppermute(single, AXES, swap_pairs)
            double, none = chunk(step, CHUNKS - 1, [(3,), (0,)], held[-1], total[1:], jnp.bfloat16)
        fresh = []
        for k in range(CHUNKS):
            rows = slice(cuts[k], cuts[k + 1])
            part = jnp.where(even, other[rows].astype(jnp.float32), 0.0)
            up = (double[rows].astype(jnp.float32) + part).astype(jnp.bfloat16)
            came = lax.ppermute(up, AXES, up_pairs)
            operands = (window, none, other, came)
            if step + 1 < steps:
                fresh.append(
                    call(
                        functools.partial(sum_kernel, cuts[k]),
                        [VMEM] * 4,
                        block(cuts[k + 1] - cuts[k]),
                        out_specs=VMEM,
                    )(*operands)
                )
            else:
                result = call(
                    functools.partial(last_kernel, step, pairs, cuts[k]),
                    [VMEM] * 4 + [ANY],
                    whole,
                    out_specs=ANY,
                    scratch_shapes=[pltpu.VMEM((cuts[k + 1] - cuts[k], width), jnp.bfloat16), pltpu.SemaphoreType.DMA],
                    input_output_aliases={4: 0},
                )(*operands, result)
        if step + 1 == steps:
            break
        held = [lax.ppermute(rows, AXES, next_pairs) for rows in fresh]
        operands = fresh + ([] if result is None else [result])
        result = call(
            functools.partial(write_kernel, step, cuts, pairs),
            [VMEM] * CHUNKS + [ANY] * (len(operands) - CHUNKS),
            whole,
            out_specs=ANY,
            scratch_shapes=[pltpu.SemaphoreType.DMA((CHUNKS,))],
            input_output_aliases={} if result is None else {CHUNKS: 0},
        )(*operands)
    return result


def solution(mesh):
    in_specs = (
        P(None, "sector", None, None),
        P("site", None, "sector", None, None),
        P("site", None, None, "sector", None, None),
        P(),
        P("site", None, "sector"),
    )
    out_specs = P("site", None, "sector", None, None)
    return jax.shard_map(per_device, mesh=mesh, in_specs=in_specs, out_specs=out_specs, check_vma=False)
```

```python
import functools

import jax
import jax.numpy as jnp
from jax import lax
from jax.experimental import pallas as pl
from jax.experimental.pallas import tpu as pltpu
from jax.sharding import PartitionSpec as P

PARTS = (11, 11, 10)
CHUNKS = len(PARTS)
AXES = ("site", "sector")
LIMIT = 20 << 20
OPEN_LIMIT = 20 << 20
SMEM = pl.BlockSpec(memory_space=pltpu.SMEM)
VMEM = pl.BlockSpec(memory_space=pltpu.VMEM)
ANY = pl.BlockSpec(memory_space=pl.ANY)


def bounds(width):
    tiles = width // 16
    ends = [sum(PARTS[:k]) * tiles // sum(PARTS) for k in range(len(PARTS) + 1)]
    return [16 * end for end in ends]


def across(a, b):
    return lax.dot_general(a, b, (((1,), (0,)), ((), ())), preferred_element_type=jnp.float32)


def down(a, b):
    return lax.dot_general(a, b, (((0,), (0,)), ((), ())), preferred_element_type=jnp.float32)


def inside(shape, row, used):
    rows = lax.broadcasted_iota(jnp.int32, shape, 0) + row
    lanes = lax.broadcasted_iota(jnp.int32, shape, 1)
    return jnp.logical_and(rows < used, lanes < used)


def pair_of(step, pairs):
    return jnp.clip(step - lax.axis_index("site"), 0, pairs - 1)


def cut(block, row, dims):
    used = dims[0, lax.axis_index("sector")]
    return jnp.where(inside(block.shape, row, used), block.astype(jnp.float32), 0.0).astype(jnp.bfloat16)


def product(e, ket_block, bra_rows, flag):
    moved = across(e, ket_block) * flag
    return down(bra_rows, moved.astype(jnp.bfloat16))


def group(states, e, row, ket, bra, flags, pair, total):
    rows = slice(row, row + e.shape[0])
    for s in states:
        part = product(e, ket[0, pair, s, 0], bra[0, s, 0, rows], flags[s, :1])
        total = part if total is None else total + part
    return total


def open_kernel(first, later, dims, flags, env, ket, bra, out, e_out, ket_out, bra_out, env_buf, ket_buf, bra_buf, sems):
    pair = pair_of(0, ket.shape[1])
    copies = [pltpu.make_async_copy(env.at[0, 0], env_buf, sems.at[0])]
    for states, kets, bras in ((first, ket_buf, bra_buf), (later, ket_out, bra_out)):
        for i, s in enumerate(states):
            copies.append(pltpu.make_async_copy(ket.at[0, pair, s, 0], kets.at[i], sems.at[len(copies)]))
            copies.append(pltpu.make_async_copy(bra.at[0, s, 0], bras.at[i], sems.at[len(copies)]))
    for copy in copies:
        copy.start()
    copies[0].wait()
    e = cut(env_buf[...], 0, dims)
    e_out[...] = e
    total = None
    for i, s in enumerate(first):
        copies[1 + 2 * i].wait()
        copies[2 + 2 * i].wait()
        part = product(e, ket_buf[i], bra_buf[i], flags[s].astype(jnp.float32))
        total = part if total is None else total + part
    out[...] = total.astype(jnp.bfloat16)
    for copy in copies[1 + 2 * len(first) :]:
        copy.wait()


def follow_kernel(later, flags, e, kets, bras, *outs):
    for i, (s, out) in enumerate(zip(later, outs)):
        out[...] = product(e[...], kets[i], bras[i], flags[s].astype(jnp.float32)).astype(jnp.bfloat16)


def setup_kernel(dims, flags, env, after, window, flag_rows, entering):
    del after
    used = dims[lax.axis_index("site") + 1, lax.axis_index("sector")]
    window[...] = jnp.where(inside(window.shape, 0, used), 1.0, 0.0).astype(window.dtype)
    for s in range(flag_rows.shape[0]):
        flag_rows[s] = jnp.zeros(flag_rows.shape[1:], jnp.float32) + flags[s].astype(jnp.float32)
    for p in range(entering.shape[0]):
        entering[p] = cut(env[p + 1, 0], 0, dims)


def step_kernel(step, row, fresh, added, groups, flags, *refs):
    refs = list(refs)
    entering = refs.pop(0) if fresh else None
    held, ket, bra = refs[:3]
    before = refs[3 : 3 + len(groups)] if added else [None] * len(groups)
    outs = refs[3 + len(groups) * added :]
    pair = pair_of(step, ket.shape[1])
    e = held[...]
    if fresh:
        e = jnp.where(lax.axis_index("site") == 0, entering[step - 1, row : row + e.shape[0]], e)
    for states, start, out in zip(groups, before, outs):
        total = group(states, e, row, ket, bra, flags, pair, None if start is None else start[...])
        out[...] = total.astype(out.dtype)


def summed(row, window, none, other, came):
    rows = slice(row, row + came.shape[0])
    sector = lax.axis_index("sector")
    total = none[rows].astype(jnp.float32)
    total = total + jnp.where(sector % 2 == 1, other[...].astype(jnp.float32), 0.0)
    total = total + jnp.where(sector >= 2, came[...].astype(jnp.float32), 0.0)
    return (total * window[rows].astype(jnp.float32)).astype(jnp.bfloat16)


def sum_kernel(row, window, none, other, came, out):
    out[...] = summed(row, window, none, other, came)


def written(pair, pairs, row, block, out, sem):
    @pl.when(jnp.logical_and(pair >= 0, pair < pairs))
    def _():
        copy = pltpu.make_async_copy(block, out.at[0, pair, 0, pl.ds(row, block.shape[0])], sem)
        copy.start()
        copy.wait()


def write_kernel(step, cuts, pairs, *refs):
    blocks = refs[: len(cuts) - 1]
    out, sems = refs[-2:]
    pair = step - lax.axis_index("site")

    @pl.when(jnp.logical_and(pair >= 0, pair < pairs))
    def _():
        copies = []
        for k, block in enumerate(blocks):
            rows = pl.ds(cuts[k], cuts[k + 1] - cuts[k])
            copies.append(pltpu.make_async_copy(block, out.at[0, pair, 0, rows], sems.at[k]))
            copies[-1].start()
        for copy in copies:
            copy.wait()


def last_kernel(step, pairs, row, window, none, other, came, before, out, block, sem):
    del before
    block[...] = summed(row, window, none, other, came)
    written(step - lax.axis_index("site"), pairs, row, block, out, sem)


def call(kernel, in_specs, out_shape, flops=0, moved=0, limit=LIMIT, **more):
    return pl.pallas_call(
        kernel,
        out_shape=out_shape,
        in_specs=in_specs,
        compiler_params=pltpu.CompilerParams(vmem_limit_bytes=limit),
        cost_estimate=pl.CostEstimate(flops=flops, bytes_accessed=moved, transcendentals=0),
        **more,
    )


def per_device(env_in, bra, ket, sector_dims, flags):
    sections = lax.axis_size("site")
    sectors = lax.axis_size("sector")
    sector = lax.axis_index("sector")
    pairs = ket.shape[1]
    width = ket.shape[-1]
    steps = pairs + sections - 1
    cuts = bounds(width)
    even = sector % 2 == 0

    def at(j, q):
        return j * sectors + q

    everyone = [(j, q) for j in range(sections) for q in range(sectors)]
    swap_pairs = [(at(j, q), at(j, q ^ 1)) for j, q in everyone]

    def swapped(rows):
        return [lax.ppermute(rows[cuts[k] : cuts[k + 1]], AXES, swap_pairs) for k in range(CHUNKS)]

    def working(step):
        return [step - p for p in range(pairs) if 0 <= step - p < sections]

    def up_pairs(step):
        work = working(step)
        if step + 1 == steps:
            return [(at(j, q), at(j, q + 2)) for j in work for q in range(sectors - 2)]
        half = sections // 2
        if sections != 4 or len({j % half for j in work}) != len(work) or 1 in work:
            return [(at(j, q), at(j, (q + 2) % sectors)) for j, q in everyone]
        found = []
        for j in range(half):
            up, back = (j + half, j) if j + half in work else (j, j + half)
            found += [(at(up, q), at(up, q + 2)) for q in range(sectors - 2)]
            found += [(at(back, q + 2), at(back, q)) for q in range(sectors - 2)]
            found += [(at(up, q), at(back, q)) for q in (sectors - 2, sectors - 1)]
            found += [(at(back, q), at(up, q)) for q in (0, 1)]
        return found

    def next_pairs(step):
        moves = [j for j in working(step) if j + 1 < sections]
        if sections == 4 and 1 not in moves:
            return [(at(j, q), at(j ^ 1, q)) for j in range(sections) for q in range(sectors)]
        return [(at(j, q), at((j + 1) % sections, q)) for j in range(sections) for q in range(sectors)]

    def block(rows, dtype=jnp.bfloat16):
        return jax.ShapeDtypeStruct((rows, width), dtype)

    def chunk(step, k, groups, held, before, dtype):
        fresh = step < pairs
        operands = [flag_rows] + ([entering] if fresh else []) + [held, ket, bra] + before
        return call(
            functools.partial(step_kernel, step, cuts[k], fresh, len(before) > 0, groups),
            [VMEM] * len(operands),
            [block(width, dtype)] * len(groups),
            4 * sum(len(states) for states in groups) * (cuts[k + 1] - cuts[k]) * width**2,
            out_specs=[VMEM] * len(groups),
        )(*operands)

    flag_here = flags.reshape(flags.shape[1])
    whole = jax.ShapeDtypeStruct((1, pairs, 1, width, width), jnp.bfloat16)
    result = None
    held = None
    for step in range(steps):
        if step == 0:
            first, later = (1, 2), (3, 0)
            copies = 1 + 2 * len(first) + 2 * len(later)
            stack = lambda n: jax.ShapeDtypeStruct((n, width, width), jnp.bfloat16)
            single, e, kets, bras = call(
                functools.partial(open_kernel, first, later),
                [SMEM, SMEM] + [pl.BlockSpec(memory_space=pltpu.HBM)] * 3,
                [block(width), block(width), stack(len(later)), stack(len(later))],
                4 * len(first) * width**3,
                limit=OPEN_LIMIT,
                scratch_shapes=[
                    pltpu.VMEM((width, width), jnp.bfloat16),
                    pltpu.VMEM((len(first), width, width), jnp.bfloat16),
                    pltpu.VMEM((len(first), width, width), jnp.bfloat16),
                    pltpu.SemaphoreType.DMA((copies,)),
                ],
                out_specs=[VMEM] * 4,
            )(*[pltpu.with_memory_space_constraint(a, pltpu.HBM) for a in (sector_dims, flag_here, env_in, ket, bra)])
            other = swapped(single)
            double, none = call(
                functools.partial(follow_kernel, later),
                [SMEM] + [VMEM] * 3,
                [block(width)] * 2,
                4 * len(later) * width**3,
                out_specs=[VMEM] * 2,
            )(flag_here, e, kets, bras)
            window, flag_rows, entering = call(
                setup_kernel,
                [SMEM, SMEM, VMEM, ANY],
                [
                    block(width),
                    jax.ShapeDtypeStruct((ket.shape[2], 8, width), jnp.float32),
                    jax.ShapeDtypeStruct((max(pairs - 1, 1), width, width), jnp.bfloat16),
                ],
                out_specs=[VMEM] * 3,
            )(sector_dims, flag_here, env_in, double)
        else:
            total = []
            for k in range(CHUNKS - 1):
                total = chunk(step, k, [(1, 2), (3,), (0,)], held[k], list(total), jnp.float32)
            total = list(total)
            (single,) = chunk(step, CHUNKS - 1, [(1, 2)], held[-1], total[:1], jnp.bfloat16)
            other = swapped(single)
            double, none = chunk(step, CHUNKS - 1, [(3,), (0,)], held[-1], total[1:], jnp.bfloat16)
        fresh = []
        for k in range(CHUNKS):
            rows = slice(cuts[k], cuts[k + 1])
            part = jnp.where(even, other[k].astype(jnp.float32), 0.0)
            up = (double[rows].astype(jnp.float32) + part).astype(jnp.bfloat16)
            came = lax.ppermute(up, AXES, up_pairs(step))
            operands = (window, none, other[k], came)
            if step + 1 < steps:
                fresh.append(
                    call(
                        functools.partial(sum_kernel, cuts[k]),
                        [VMEM] * 4,
                        block(cuts[k + 1] - cuts[k]),
                        out_specs=VMEM,
                    )(*operands)
                )
            else:
                result = call(
                    functools.partial(last_kernel, step, pairs, cuts[k]),
                    [VMEM] * 4 + [ANY],
                    whole,
                    out_specs=ANY,
                    scratch_shapes=[pltpu.VMEM((cuts[k + 1] - cuts[k], width), jnp.bfloat16), pltpu.SemaphoreType.DMA],
                    input_output_aliases={4: 0},
                )(*operands, result)
        if step + 1 == steps:
            break
        held = [lax.ppermute(rows, AXES, next_pairs(step)) for rows in fresh]
        operands = fresh + ([] if result is None else [result])
        result = call(
            functools.partial(write_kernel, step, cuts, pairs),
            [VMEM] * CHUNKS + [ANY] * (len(operands) - CHUNKS),
            whole,
            out_specs=ANY,
            scratch_shapes=[pltpu.SemaphoreType.DMA((CHUNKS,))],
            input_output_aliases={} if result is None else {CHUNKS: 0},
        )(*operands)
    return result


def solution(mesh):
    in_specs = (
        P(None, "sector", None, None),
        P("site", None, "sector", None, None),
        P("site", None, None, "sector", None, None),
        P(),
        P("site", None, "sector"),
    )
    out_specs = P("site", None, "sector", None, None)
    return jax.shard_map(per_device, mesh=mesh, in_specs=in_specs, out_specs=out_specs, check_vma=False)
```

```python
import functools

import jax
import jax.numpy as jnp
from jax import lax
from jax.experimental import pallas as pl
from jax.experimental.pallas import tpu as pltpu
from jax.sharding import PartitionSpec as P

PARTS = (10, 11, 11)
CHUNKS = len(PARTS)
LAST_PARTS = (21, 11)
AXES = ("site", "sector")
LIMIT = 20 << 20
OPEN_LIMIT = 20 << 20
SMEM = pl.BlockSpec(memory_space=pltpu.SMEM)
VMEM = pl.BlockSpec(memory_space=pltpu.VMEM)
ANY = pl.BlockSpec(memory_space=pl.ANY)


def bounds(width, parts):
    tiles = width // 16
    ends = [sum(parts[:k]) * tiles // sum(parts) for k in range(len(parts) + 1)]
    return [16 * end for end in ends]


def across(a, b):
    return lax.dot_general(a, b, (((1,), (0,)), ((), ())), preferred_element_type=jnp.float32)


def down(a, b):
    return lax.dot_general(a, b, (((0,), (0,)), ((), ())), preferred_element_type=jnp.float32)


def inside(shape, row, used):
    rows = lax.broadcasted_iota(jnp.int32, shape, 0) + row
    lanes = lax.broadcasted_iota(jnp.int32, shape, 1)
    return jnp.logical_and(rows < used, lanes < used)


def pair_of(step, pairs):
    return jnp.clip(step - lax.axis_index("site"), 0, pairs - 1)


def cut(block, row, dims):
    used = dims[0, lax.axis_index("sector")]
    return jnp.where(inside(block.shape, row, used), block.astype(jnp.float32), 0.0).astype(jnp.bfloat16)


def product(e, ket_block, bra_rows, flag):
    moved = across(e, ket_block) * flag
    return down(bra_rows, moved.astype(jnp.bfloat16))


def group(states, e, row, ket, bra, flags, pair, total):
    rows = slice(row, row + e.shape[0])
    for s in states:
        part = product(e, ket[0, pair, s, 0], bra[0, s, 0, rows], flags[s, :1])
        total = part if total is None else total + part
    return total


def parted(total, cuts, outs):
    for start, end, out in zip(cuts, cuts[1:], outs):
        out[...] = total[start:end].astype(out.dtype)


def open_kernel(first, later, cuts, dims_in, flags_in, env, ket, bra, *refs):
    outs, (e_out, block_out, flag_rows, dims, flags, env_buf, ket_buf, bra_buf, small_sems, sems) = refs[: len(cuts) - 1], refs[len(cuts) - 1 :]
    ket_out, bra_out = block_out.at[: len(later)], block_out.at[len(later) :]
    pair = pair_of(0, ket.shape[1])
    copies = [pltpu.make_async_copy(env.at[0, 0], env_buf, sems.at[0])]
    for states, kets, bras in ((first, ket_buf, bra_buf), (later, ket_out, bra_out)):
        for i, s in enumerate(states):
            copies.append(pltpu.make_async_copy(ket.at[0, pair, s, 0], kets.at[i], sems.at[len(copies)]))
            copies.append(pltpu.make_async_copy(bra.at[0, s, 0], bras.at[i], sems.at[len(copies)]))
    soon = 1 + 2 * len(first)
    small = [
        pltpu.make_async_copy(dims_in, dims, small_sems.at[0]),
        pltpu.make_async_copy(flags_in, flags, small_sems.at[1]),
    ]
    for copy in small:
        copy.start()
    for copy in copies[:soon]:
        copy.start()
    for copy in small:
        copy.wait()
    copies[0].wait()
    for copy in copies[soon:]:
        copy.start()
    e = cut(env_buf[...], 0, dims)
    e_out[...] = e
    for s in range(flag_rows.shape[0]):
        flag_rows[s] = jnp.zeros(flag_rows.shape[1:], jnp.float32) + flags[s].astype(jnp.float32)
    total = None
    for i, s in enumerate(first):
        copies[1 + 2 * i].wait()
        copies[2 + 2 * i].wait()
        part = product(e, ket_buf[i], bra_buf[i], flags[s].astype(jnp.float32))
        total = part if total is None else total + part
    parted(total, cuts, outs)
    for copy in copies[1 + 2 * len(first) :]:
        copy.wait()


def follow_kernel(later, flags, e, blocks, *outs):
    for i, (s, out) in enumerate(zip(later, outs)):
        out[...] = product(e[...], blocks[i], blocks[len(later) + i], flags[s, :1]).astype(jnp.bfloat16)


def setup_kernel(dims, env, after, window, entering):
    del after
    used = dims[lax.axis_index("site") + 1, lax.axis_index("sector")]
    window[...] = jnp.where(inside(window.shape, 0, used), 1.0, 0.0).astype(window.dtype)
    for p in range(entering.shape[0]):
        entering[p] = cut(env[p + 1, 0], 0, dims)


def step_kernel(step, row, fresh, added, groups, cuts, flags, *refs):
    refs = list(refs)
    entering = refs.pop(0) if fresh else None
    held, ket, bra = refs[:3]
    before = refs[3 : 3 + len(groups)] if added else [None] * len(groups)
    outs = refs[3 + len(groups) * added :]
    pair = pair_of(step, ket.shape[1])
    e = held[...]
    if fresh:
        e = jnp.where(lax.axis_index("site") == 0, entering[step - 1, row : row + e.shape[0]], e)
    for states, start, out in zip(groups, before, outs):
        total = group(states, e, row, ket, bra, flags, pair, None if start is None else start[...])
        if cuts is None:
            out[...] = total.astype(out.dtype)
        else:
            parted(total, cuts, outs)


def summed(row, window, none, other, came):
    rows = slice(row, row + came.shape[0])
    sector = lax.axis_index("sector")
    total = none[rows].astype(jnp.float32)
    total = total + jnp.where(sector % 2 == 1, other[...].astype(jnp.float32), 0.0)
    total = total + jnp.where(sector >= 2, came[...].astype(jnp.float32), 0.0)
    return (total * window[rows].astype(jnp.float32)).astype(jnp.bfloat16)


def sum_kernel(row, window, none, other, came, out):
    out[...] = summed(row, window, none, other, came)


def written(pair, pairs, row, block, out, sem):
    @pl.when(jnp.logical_and(pair >= 0, pair < pairs))
    def _():
        copy = pltpu.make_async_copy(block, out.at[0, pair, 0, pl.ds(row, block.shape[0])], sem)
        copy.start()
        copy.wait()


def write_kernel(step, cuts, pairs, *refs):
    blocks = refs[: len(cuts) - 1]
    out, sems = refs[-2:]
    pair = step - lax.axis_index("site")

    @pl.when(jnp.logical_and(pair >= 0, pair < pairs))
    def _():
        copies = []
        for k, block in enumerate(blocks):
            rows = pl.ds(cuts[k], cuts[k + 1] - cuts[k])
            copies.append(pltpu.make_async_copy(block, out.at[0, pair, 0, rows], sems.at[k]))
            copies[-1].start()
        for copy in copies:
            copy.wait()


def last_kernel(step, pairs, row, window, none, other, came, before, out, block, sem):
    del before
    block[...] = summed(row, window, none, other, came)
    written(step - lax.axis_index("site"), pairs, row, block, out, sem)


def call(kernel, in_specs, out_shape, flops=0, moved=0, limit=LIMIT, **more):
    return pl.pallas_call(
        kernel,
        out_shape=out_shape,
        in_specs=in_specs,
        compiler_params=pltpu.CompilerParams(vmem_limit_bytes=limit),
        cost_estimate=pl.CostEstimate(flops=flops, bytes_accessed=moved, transcendentals=0),
        **more,
    )


def per_device(env_in, bra, ket, sector_dims, flags):
    sections = lax.axis_size("site")
    sectors = lax.axis_size("sector")
    sector = lax.axis_index("sector")
    pairs = ket.shape[1]
    width = ket.shape[-1]
    steps = pairs + sections - 1
    cuts = bounds(width, PARTS)
    last_cuts = bounds(width, LAST_PARTS)
    even = sector % 2 == 0

    def at(j, q):
        return j * sectors + q

    everyone = [(j, q) for j in range(sections) for q in range(sectors)]
    swap_pairs = [(at(j, q), at(j, q ^ 1)) for j, q in everyone]

    def swapped(parts):
        return [lax.ppermute(part, AXES, swap_pairs) for part in parts]

    def working(step):
        return [step - p for p in range(pairs) if 0 <= step - p < sections]

    def up_pairs(step):
        work = working(step)
        if step + 1 == steps:
            return [(at(j, q), at(j, q + 2)) for j in work for q in range(sectors - 2)]
        half = sections // 2
        if sections != 4 or len({j % half for j in work}) != len(work) or 1 in work:
            return [(at(j, q), at(j, (q + 2) % sectors)) for j, q in everyone]
        found = []
        for j in range(half):
            up, back = (j + half, j) if j + half in work else (j, j + half)
            found += [(at(up, q), at(up, q + 2)) for q in range(sectors - 2)]
            found += [(at(back, q + 2), at(back, q)) for q in range(sectors - 2)]
            found += [(at(up, q), at(back, q)) for q in (sectors - 2, sectors - 1)]
            found += [(at(back, q), at(up, q)) for q in (0, 1)]
        return found

    def next_pairs(step):
        moves = [j for j in working(step) if j + 1 < sections]
        if sections == 4 and 1 not in moves:
            return [(at(j, q), at(j ^ 1, q)) for j in range(sections) for q in range(sectors)]
        return [(at(j, q), at((j + 1) % sections, q)) for j in range(sections) for q in range(sectors)]

    def block(rows, dtype=jnp.bfloat16):
        return jax.ShapeDtypeStruct((rows, width), dtype)

    def blocks_of(parts):
        return [block(end - start) for start, end in zip(parts, parts[1:])]

    def chunk(step, k, groups, held, before, dtype, parts=None):
        fresh = step < pairs
        operands = [flag_rows] + ([entering] if fresh else []) + [held, ket, bra] + before
        return call(
            functools.partial(step_kernel, step, cuts[k], fresh, len(before) > 0, groups, parts),
            [VMEM] * len(operands),
            [block(width, dtype)] * len(groups) if parts is None else blocks_of(parts),
            4 * sum(len(states) for states in groups) * (cuts[k + 1] - cuts[k]) * width**2,
            out_specs=[VMEM] * (len(groups) if parts is None else len(parts) - 1),
        )(*operands)

    flag_here = flags.reshape(flags.shape[1])
    whole = jax.ShapeDtypeStruct((1, pairs, 1, width, width), jnp.bfloat16)
    result = None
    held = None
    for step in range(steps):
        if step == 0:
            first, later = (1, 2), (3, 0)
            copies = 1 + 2 * len(first) + 2 * len(later)
            stack = lambda n: jax.ShapeDtypeStruct((n, width, width), jnp.bfloat16)
            *single, e, blocks, flag_rows = call(
                functools.partial(open_kernel, first, later, cuts),
                [pl.BlockSpec(memory_space=pltpu.HBM)] * 5,
                blocks_of(cuts)
                + [
                    block(width),
                    stack(2 * len(later)),
                    jax.ShapeDtypeStruct((ket.shape[2], 8, width), jnp.float32),
                ],
                4 * len(first) * width**3,
                limit=OPEN_LIMIT,
                scratch_shapes=[
                    pltpu.SMEM(sector_dims.shape, jnp.int32),
                    pltpu.SMEM(flag_here.shape, jnp.int32),
                    pltpu.VMEM((width, width), jnp.bfloat16),
                    pltpu.VMEM((len(first), width, width), jnp.bfloat16),
                    pltpu.VMEM((len(first), width, width), jnp.bfloat16),
                    pltpu.SemaphoreType.DMA((2,)),
                    pltpu.SemaphoreType.DMA((copies,)),
                ],
                out_specs=[VMEM] * (CHUNKS + 3),
            )(*[pltpu.with_memory_space_constraint(a, pltpu.HBM) for a in (sector_dims, flag_here, env_in, ket, bra)])
            other = swapped(single)
            double, none = call(
                functools.partial(follow_kernel, later),
                [VMEM] * 3,
                [block(width)] * 2,
                4 * len(later) * width**3,
                out_specs=[VMEM] * 2,
            )(flag_rows, e, blocks)
            window, entering = call(
                setup_kernel,
                [SMEM, VMEM, ANY],
                [
                    block(width),
                    jax.ShapeDtypeStruct((max(pairs - 1, 1), width, width), jnp.bfloat16),
                ],
                out_specs=[VMEM] * 2,
            )(sector_dims, env_in, double)
        else:
            total = []
            for k in range(CHUNKS - 1):
                total = chunk(step, k, [(1, 2), (3,), (0,)], held[k], list(total), jnp.float32)
            total = list(total)
            parts = cuts if step + 1 < steps else last_cuts
            single = chunk(step, CHUNKS - 1, [(1, 2)], held[-1], total[:1], jnp.bfloat16, parts)
            other = swapped(single)
            double, none = chunk(step, CHUNKS - 1, [(3,), (0,)], held[-1], total[1:], jnp.bfloat16)
        fresh = []
        if step + 1 == steps:
            cuts = last_cuts
        for k in range(len(cuts) - 1):
            rows = slice(cuts[k], cuts[k + 1])
            part = jnp.where(even, other[k].astype(jnp.float32), 0.0)
            up = (double[rows].astype(jnp.float32) + part).astype(jnp.bfloat16)
            came = lax.ppermute(up, AXES, up_pairs(step))
            operands = (window, none, other[k], came)
            if step + 1 < steps:
                fresh.append(
                    call(
                        functools.partial(sum_kernel, cuts[k]),
                        [VMEM] * 4,
                        block(cuts[k + 1] - cuts[k]),
                        out_specs=VMEM,
                    )(*operands)
                )
            else:
                result = call(
                    functools.partial(last_kernel, step, pairs, cuts[k]),
                    [VMEM] * 4 + [ANY],
                    whole,
                    out_specs=ANY,
                    scratch_shapes=[pltpu.VMEM((cuts[k + 1] - cuts[k], width), jnp.bfloat16), pltpu.SemaphoreType.DMA],
                    input_output_aliases={4: 0},
                )(*operands, result)
        if step + 1 == steps:
            break
        held = [lax.ppermute(rows, AXES, next_pairs(step)) for rows in fresh]
        operands = fresh + ([] if result is None else [result])
        result = call(
            functools.partial(write_kernel, step, cuts, pairs),
            [VMEM] * CHUNKS + [ANY] * (len(operands) - CHUNKS),
            whole,
            out_specs=ANY,
            scratch_shapes=[pltpu.SemaphoreType.DMA((CHUNKS,))],
            input_output_aliases={} if result is None else {CHUNKS: 0},
        )(*operands)
    return result


def solution(mesh):
    in_specs = (
        P(None, "sector", None, None),
        P("site", None, "sector", None, None),
        P("site", None, None, "sector", None, None),
        P(),
        P("site", None, "sector"),
    )
    out_specs = P("site", None, "sector", None, None)
    return jax.shard_map(per_device, mesh=mesh, in_specs=in_specs, out_specs=out_specs, check_vma=False)
```

```python
import functools

import jax
import jax.numpy as jnp
from jax import lax
from jax.experimental import pallas as pl
from jax.experimental.pallas import tpu as pltpu
from jax.sharding import PartitionSpec as P

PARTS = (8, 8, 8, 8)
CHUNKS = len(PARTS)
LAST_PARTS = (21, 11)
AXES = ("site", "sector")
LIMIT = 20 << 20
OPEN_LIMIT = 20 << 20
SMEM = pl.BlockSpec(memory_space=pltpu.SMEM)
VMEM = pl.BlockSpec(memory_space=pltpu.VMEM)
ANY = pl.BlockSpec(memory_space=pl.ANY)


def bounds(width, parts):
    tiles = width // 16
    ends = [sum(parts[:k]) * tiles // sum(parts) for k in range(len(parts) + 1)]
    return [16 * end for end in ends]


def across(a, b):
    return lax.dot_general(a, b, (((1,), (0,)), ((), ())), preferred_element_type=jnp.float32)


def down(a, b):
    return lax.dot_general(a, b, (((0,), (0,)), ((), ())), preferred_element_type=jnp.float32)


def inside(shape, row, used):
    rows = lax.broadcasted_iota(jnp.int32, shape, 0) + row
    lanes = lax.broadcasted_iota(jnp.int32, shape, 1)
    return jnp.logical_and(rows < used, lanes < used)


def pair_of(step, pairs):
    return jnp.clip(step - lax.axis_index("site"), 0, pairs - 1)


def cut(block, row, dims):
    used = dims[0, lax.axis_index("sector")]
    return jnp.where(inside(block.shape, row, used), block.astype(jnp.float32), 0.0).astype(jnp.bfloat16)


def product(e, ket_block, bra_rows, flag):
    moved = across(e, ket_block) * flag
    return down(bra_rows, moved.astype(jnp.bfloat16))


def group(states, e, row, ket, bra, flags, pair, total):
    rows = slice(row, row + e.shape[0])
    moved = [(across(e, ket[0, pair, s, 0]) * flags[s, :1]).astype(jnp.bfloat16) for s in states]
    blocks = [bra[0, s, 0, rows] for s in states]
    part = down(jnp.concatenate(blocks, axis=0), jnp.concatenate(moved, axis=0))
    return part if total is None else total + part


def parted(total, cuts, outs):
    for start, end, out in zip(cuts, cuts[1:], outs):
        out[...] = total[start:end].astype(out.dtype)


def open_kernel(first, later, cuts, dims_in, flags_in, env, ket, bra, *refs):
    outs, (e_out, block_out, flag_rows, dims, flags, env_buf, ket_buf, bra_buf, small_sems, sems) = refs[: len(cuts) - 1], refs[len(cuts) - 1 :]
    ket_out, bra_out = block_out.at[: len(later)], block_out.at[len(later) :]
    pair = pair_of(0, ket.shape[1])
    copies = [pltpu.make_async_copy(env.at[0, 0], env_buf, sems.at[0])]
    for states, kets, bras in ((first, ket_buf, bra_buf), (later, ket_out, bra_out)):
        for i, s in enumerate(states):
            copies.append(pltpu.make_async_copy(ket.at[0, pair, s, 0], kets.at[i], sems.at[len(copies)]))
            copies.append(pltpu.make_async_copy(bra.at[0, s, 0], bras.at[i], sems.at[len(copies)]))
    soon = 1 + 2 * len(first)
    small = [
        pltpu.make_async_copy(dims_in, dims, small_sems.at[0]),
        pltpu.make_async_copy(flags_in, flags, small_sems.at[1]),
    ]
    for copy in small:
        copy.start()
    for copy in copies[:soon]:
        copy.start()
    for copy in small:
        copy.wait()
    copies[0].wait()
    for copy in copies[soon:]:
        copy.start()
    e = cut(env_buf[...], 0, dims)
    e_out[...] = e
    for s in range(flag_rows.shape[0]):
        flag_rows[s] = jnp.zeros(flag_rows.shape[1:], jnp.float32) + flags[s].astype(jnp.float32)
    total = None
    for i, s in enumerate(first):
        copies[1 + 2 * i].wait()
        copies[2 + 2 * i].wait()
        part = product(e, ket_buf[i], bra_buf[i], flags[s].astype(jnp.float32))
        total = part if total is None else total + part
    parted(total, cuts, outs)
    for copy in copies[1 + 2 * len(first) :]:
        copy.wait()


def follow_kernel(later, flags, e, blocks, *outs):
    for i, (s, out) in enumerate(zip(later, outs)):
        out[...] = product(e[...], blocks[i], blocks[len(later) + i], flags[s, :1]).astype(jnp.bfloat16)


def setup_kernel(dims, env, after, window, entering):
    del after
    used = dims[lax.axis_index("site") + 1, lax.axis_index("sector")]
    window[...] = jnp.where(inside(window.shape, 0, used), 1.0, 0.0).astype(window.dtype)
    for p in range(entering.shape[0]):
        entering[p] = cut(env[p + 1, 0], 0, dims)


def step_kernel(step, row, fresh, added, groups, cuts, flags, *refs):
    refs = list(refs)
    entering = refs.pop(0) if fresh else None
    held, ket, bra = refs[:3]
    before = refs[3 : 3 + len(groups)] if added else [None] * len(groups)
    outs = refs[3 + len(groups) * added :]
    pair = pair_of(step, ket.shape[1])
    e = held[...]
    if fresh:
        e = jnp.where(lax.axis_index("site") == 0, entering[step - 1, row : row + e.shape[0]], e)
    for states, start, out in zip(groups, before, outs):
        total = group(states, e, row, ket, bra, flags, pair, None if start is None else start[...])
        if cuts is None:
            out[...] = total.astype(out.dtype)
        else:
            parted(total, cuts, outs)


def summed(row, window, none, other, came):
    rows = slice(row, row + came.shape[0])
    sector = lax.axis_index("sector")
    total = none[rows].astype(jnp.float32)
    total = total + jnp.where(sector % 2 == 1, other[...].astype(jnp.float32), 0.0)
    total = total + jnp.where(sector >= 2, came[...].astype(jnp.float32), 0.0)
    return (total * window[rows].astype(jnp.float32)).astype(jnp.bfloat16)


def sum_kernel(row, window, none, other, came, out):
    out[...] = summed(row, window, none, other, came)


def written(pair, pairs, row, block, out, sem):
    @pl.when(jnp.logical_and(pair >= 0, pair < pairs))
    def _():
        copy = pltpu.make_async_copy(block, out.at[0, pair, 0, pl.ds(row, block.shape[0])], sem)
        copy.start()
        copy.wait()


def write_kernel(step, cuts, pairs, *refs):
    blocks = refs[: len(cuts) - 1]
    out, sems = refs[-2:]
    pair = step - lax.axis_index("site")

    @pl.when(jnp.logical_and(pair >= 0, pair < pairs))
    def _():
        copies = []
        for k, block in enumerate(blocks):
            rows = pl.ds(cuts[k], cuts[k + 1] - cuts[k])
            copies.append(pltpu.make_async_copy(block, out.at[0, pair, 0, rows], sems.at[k]))
            copies[-1].start()
        for copy in copies:
            copy.wait()


def last_kernel(step, pairs, row, window, none, other, came, before, out, block, sem):
    del before
    block[...] = summed(row, window, none, other, came)
    written(step - lax.axis_index("site"), pairs, row, block, out, sem)


def call(kernel, in_specs, out_shape, flops=0, moved=0, limit=LIMIT, **more):
    return pl.pallas_call(
        kernel,
        out_shape=out_shape,
        in_specs=in_specs,
        compiler_params=pltpu.CompilerParams(vmem_limit_bytes=limit),
        cost_estimate=pl.CostEstimate(flops=flops, bytes_accessed=moved, transcendentals=0),
        **more,
    )


def per_device(env_in, bra, ket, sector_dims, flags):
    sections = lax.axis_size("site")
    sectors = lax.axis_size("sector")
    sector = lax.axis_index("sector")
    pairs = ket.shape[1]
    width = ket.shape[-1]
    steps = pairs + sections - 1
    cuts = bounds(width, PARTS)
    last_cuts = bounds(width, LAST_PARTS)
    even = sector % 2 == 0

    def at(j, q):
        return j * sectors + q

    everyone = [(j, q) for j in range(sections) for q in range(sectors)]
    swap_pairs = [(at(j, q), at(j, q ^ 1)) for j, q in everyone]

    def swapped(parts):
        return [lax.ppermute(part, AXES, swap_pairs) for part in parts]

    def working(step):
        return [step - p for p in range(pairs) if 0 <= step - p < sections]

    def up_pairs(step):
        work = working(step)
        if step + 1 == steps:
            return [(at(j, q), at(j, q + 2)) for j in work for q in range(sectors - 2)]
        half = sections // 2
        if sections != 4 or len({j % half for j in work}) != len(work) or 1 in work:
            return [(at(j, q), at(j, (q + 2) % sectors)) for j, q in everyone]
        found = []
        for j in range(half):
            up, back = (j + half, j) if j + half in work else (j, j + half)
            found += [(at(up, q), at(up, q + 2)) for q in range(sectors - 2)]
            found += [(at(back, q + 2), at(back, q)) for q in range(sectors - 2)]
            found += [(at(up, q), at(back, q)) for q in (sectors - 2, sectors - 1)]
            found += [(at(back, q), at(up, q)) for q in (0, 1)]
        return found

    def next_pairs(step):
        moves = [j for j in working(step) if j + 1 < sections]
        if sections == 4 and 1 not in moves:
            return [(at(j, q), at(j ^ 1, q)) for j in range(sections) for q in range(sectors)]
        return [(at(j, q), at((j + 1) % sections, q)) for j in range(sections) for q in range(sectors)]

    def block(rows, dtype=jnp.bfloat16):
        return jax.ShapeDtypeStruct((rows, width), dtype)

    def blocks_of(parts):
        return [block(end - start) for start, end in zip(parts, parts[1:])]

    def chunk(step, k, groups, held, before, dtype, parts=None):
        fresh = step < pairs
        operands = [flag_rows] + ([entering] if fresh else []) + [held, ket, bra] + before
        return call(
            functools.partial(step_kernel, step, cuts[k], fresh, len(before) > 0, groups, parts),
            [VMEM] * len(operands),
            [block(width, dtype)] * len(groups) if parts is None else blocks_of(parts),
            4 * sum(len(states) for states in groups) * (cuts[k + 1] - cuts[k]) * width**2,
            out_specs=[VMEM] * (len(groups) if parts is None else len(parts) - 1),
        )(*operands)

    flag_here = flags.reshape(flags.shape[1])
    whole = jax.ShapeDtypeStruct((1, pairs, 1, width, width), jnp.bfloat16)
    result = None
    held = None
    for step in range(steps):
        if step == 0:
            first, later = (1, 2), (3, 0)
            copies = 1 + 2 * len(first) + 2 * len(later)
            stack = lambda n: jax.ShapeDtypeStruct((n, width, width), jnp.bfloat16)
            *single, e, blocks, flag_rows = call(
                functools.partial(open_kernel, first, later, cuts),
                [pl.BlockSpec(memory_space=pltpu.HBM)] * 5,
                blocks_of(cuts)
                + [
                    block(width),
                    stack(2 * len(later)),
                    jax.ShapeDtypeStruct((ket.shape[2], 8, width), jnp.float32),
                ],
                4 * len(first) * width**3,
                limit=OPEN_LIMIT,
                scratch_shapes=[
                    pltpu.SMEM(sector_dims.shape, jnp.int32),
                    pltpu.SMEM(flag_here.shape, jnp.int32),
                    pltpu.VMEM((width, width), jnp.bfloat16),
                    pltpu.VMEM((len(first), width, width), jnp.bfloat16),
                    pltpu.VMEM((len(first), width, width), jnp.bfloat16),
                    pltpu.SemaphoreType.DMA((2,)),
                    pltpu.SemaphoreType.DMA((copies,)),
                ],
                out_specs=[VMEM] * (CHUNKS + 3),
            )(*[pltpu.with_memory_space_constraint(a, pltpu.HBM) for a in (sector_dims, flag_here, env_in, ket, bra)])
            other = swapped(single)
            double, none = call(
                functools.partial(follow_kernel, later),
                [VMEM] * 3,
                [block(width)] * 2,
                4 * len(later) * width**3,
                out_specs=[VMEM] * 2,
            )(flag_rows, e, blocks)
            window, entering = call(
                setup_kernel,
                [SMEM, VMEM, ANY],
                [
                    block(width),
                    jax.ShapeDtypeStruct((max(pairs - 1, 1), width, width), jnp.bfloat16),
                ],
                out_specs=[VMEM] * 2,
            )(sector_dims, env_in, double)
        else:
            total = []
            for k in range(CHUNKS - 1):
                total = chunk(step, k, [(1, 2), (3,), (0,)], held[k], list(total), jnp.float32)
            total = list(total)
            parts = cuts if step + 1 < steps else last_cuts
            single = chunk(step, CHUNKS - 1, [(1, 2)], held[-1], total[:1], jnp.bfloat16, parts)
            other = swapped(single)
            double, none = chunk(step, CHUNKS - 1, [(3,), (0,)], held[-1], total[1:], jnp.bfloat16)
        fresh = []
        if step + 1 == steps:
            cuts = last_cuts
        for k in range(len(cuts) - 1):
            rows = slice(cuts[k], cuts[k + 1])
            part = jnp.where(even, other[k].astype(jnp.float32), 0.0)
            up = (double[rows].astype(jnp.float32) + part).astype(jnp.bfloat16)
            came = lax.ppermute(up, AXES, up_pairs(step))
            operands = (window, none, other[k], came)
            if step + 1 < steps:
                fresh.append(
                    call(
                        functools.partial(sum_kernel, cuts[k]),
                        [VMEM] * 4,
                        block(cuts[k + 1] - cuts[k]),
                        out_specs=VMEM,
                    )(*operands)
                )
            else:
                result = call(
                    functools.partial(last_kernel, step, pairs, cuts[k]),
                    [VMEM] * 4 + [ANY],
                    whole,
                    out_specs=ANY,
                    scratch_shapes=[pltpu.VMEM((cuts[k + 1] - cuts[k], width), jnp.bfloat16), pltpu.SemaphoreType.DMA],
                    input_output_aliases={4: 0},
                )(*operands, result)
        if step + 1 == steps:
            break
        held = [lax.ppermute(rows, AXES, next_pairs(step)) for rows in fresh]
        operands = fresh + ([] if result is None else [result])
        result = call(
            functools.partial(write_kernel, step, cuts, pairs),
            [VMEM] * CHUNKS + [ANY] * (len(operands) - CHUNKS),
            whole,
            out_specs=ANY,
            scratch_shapes=[pltpu.SemaphoreType.DMA((CHUNKS,))],
            input_output_aliases={} if result is None else {CHUNKS: 0},
        )(*operands)
    return result


def solution(mesh):
    in_specs = (
        P(None, "sector", None, None),
        P("site", None, "sector", None, None),
        P("site", None, None, "sector", None, None),
        P(),
        P("site", None, "sector"),
    )
    out_specs = P("site", None, "sector", None, None)
    return jax.shard_map(per_device, mesh=mesh, in_specs=in_specs, out_specs=out_specs, check_vma=False)
```

```python
import functools

import jax
import jax.numpy as jnp
from jax import lax
from jax.experimental import pallas as pl
from jax.experimental.pallas import tpu as pltpu
from jax.sharding import PartitionSpec as P

PARTS = (8, 8, 8, 8)
CHUNKS = len(PARTS)
JOINED = (0, 2, 3)
LAST_PARTS = (21, 11)
AXES = ("site", "sector")
LIMIT = 20 << 20
OPEN_LIMIT = 20 << 20
SMEM = pl.BlockSpec(memory_space=pltpu.SMEM)
VMEM = pl.BlockSpec(memory_space=pltpu.VMEM)
ANY = pl.BlockSpec(memory_space=pl.ANY)


def bounds(width, parts):
    tiles = width // 16
    ends = [sum(parts[:k]) * tiles // sum(parts) for k in range(len(parts) + 1)]
    return [16 * end for end in ends]


def across(a, b):
    return lax.dot_general(a, b, (((1,), (0,)), ((), ())), preferred_element_type=jnp.float32)


def down(a, b):
    return lax.dot_general(a, b, (((0,), (0,)), ((), ())), preferred_element_type=jnp.float32)


def inside(shape, row, used):
    rows = lax.broadcasted_iota(jnp.int32, shape, 0) + row
    lanes = lax.broadcasted_iota(jnp.int32, shape, 1)
    return jnp.logical_and(rows < used, lanes < used)


def pair_of(step, pairs):
    return jnp.clip(step - lax.axis_index("site"), 0, pairs - 1)


def cut(block, row, dims):
    used = dims[0, lax.axis_index("sector")]
    return jnp.where(inside(block.shape, row, used), block.astype(jnp.float32), 0.0).astype(jnp.bfloat16)


def product(e, ket_block, bra_rows, flag):
    moved = across(e, ket_block) * flag
    return down(bra_rows, moved.astype(jnp.bfloat16))


def group(states, e, row, ket, bra, flags, pair, total):
    rows = slice(row, row + e.shape[0])
    moved = [(across(e, ket[0, pair, s, 0]) * flags[s, :1]).astype(jnp.bfloat16) for s in states]
    blocks = [bra[0, s, 0, rows] for s in states]
    part = down(jnp.concatenate(blocks, axis=0), jnp.concatenate(moved, axis=0))
    return part if total is None else total + part


def parted(total, cuts, outs):
    for start, end, out in zip(cuts, cuts[1:], outs):
        out[...] = total[start:end].astype(out.dtype)


def open_kernel(first, later, cuts, dims_in, flags_in, env, ket, bra, *refs):
    outs, (e_out, block_out, flag_rows, dims, flags, env_buf, ket_buf, bra_buf, small_sems, sems) = refs[: len(cuts) - 1], refs[len(cuts) - 1 :]
    ket_out, bra_out = block_out.at[: len(later)], block_out.at[len(later) :]
    pair = pair_of(0, ket.shape[1])
    copies = [pltpu.make_async_copy(env.at[0, 0], env_buf, sems.at[0])]
    for states, kets, bras in ((first, ket_buf, bra_buf), (later, ket_out, bra_out)):
        for i, s in enumerate(states):
            copies.append(pltpu.make_async_copy(ket.at[0, pair, s, 0], kets.at[i], sems.at[len(copies)]))
            copies.append(pltpu.make_async_copy(bra.at[0, s, 0], bras.at[i], sems.at[len(copies)]))
    soon = 1 + 2 * len(first)
    small = [
        pltpu.make_async_copy(dims_in, dims, small_sems.at[0]),
        pltpu.make_async_copy(flags_in, flags, small_sems.at[1]),
    ]
    for copy in small:
        copy.start()
    for copy in copies[:soon]:
        copy.start()
    for copy in small:
        copy.wait()
    copies[0].wait()
    for copy in copies[soon:]:
        copy.start()
    e = cut(env_buf[...], 0, dims)
    e_out[...] = e
    for s in range(flag_rows.shape[0]):
        flag_rows[s] = jnp.zeros(flag_rows.shape[1:], jnp.float32) + flags[s].astype(jnp.float32)
    total = None
    for i, s in enumerate(first):
        copies[1 + 2 * i].wait()
        copies[2 + 2 * i].wait()
        part = product(e, ket_buf[i], bra_buf[i], flags[s].astype(jnp.float32))
        total = part if total is None else total + part
    parted(total, cuts, outs)
    for copy in copies[1 + 2 * len(first) :]:
        copy.wait()


def follow_kernel(later, flags, e, blocks, *outs):
    for i, (s, out) in enumerate(zip(later, outs)):
        out[...] = product(e[...], blocks[i], blocks[len(later) + i], flags[s, :1]).astype(jnp.bfloat16)


def setup_kernel(dims, env, after, window, entering):
    del after
    used = dims[lax.axis_index("site") + 1, lax.axis_index("sector")]
    window[...] = jnp.where(inside(window.shape, 0, used), 1.0, 0.0).astype(window.dtype)
    for p in range(entering.shape[0]):
        entering[p] = cut(env[p + 1, 0], 0, dims)


def step_kernel(step, row, count, fresh, added, groups, cuts, flags, *refs):
    refs = list(refs)
    entering = refs.pop(0) if fresh else None
    held, (ket, bra) = refs[:count], refs[count : count + 2]
    refs = refs[count + 2 :]
    before = refs[: len(groups)] if added else [None] * len(groups)
    outs = refs[len(groups) * added :]
    pair = pair_of(step, ket.shape[1])
    e = jnp.concatenate([rows[...] for rows in held], axis=0)
    if fresh:
        e = jnp.where(lax.axis_index("site") == 0, entering[step - 1, row : row + e.shape[0]], e)
    for states, start, out in zip(groups, before, outs):
        total = group(states, e, row, ket, bra, flags, pair, None if start is None else start[...])
        if cuts is None:
            out[...] = total.astype(out.dtype)
        else:
            parted(total, cuts, outs)


def summed(row, window, none, other, came):
    rows = slice(row, row + came.shape[0])
    sector = lax.axis_index("sector")
    total = none[rows].astype(jnp.float32)
    total = total + jnp.where(sector % 2 == 1, other[...].astype(jnp.float32), 0.0)
    total = total + jnp.where(sector >= 2, came[...].astype(jnp.float32), 0.0)
    return (total * window[rows].astype(jnp.float32)).astype(jnp.bfloat16)


def sum_kernel(row, window, none, other, came, out):
    out[...] = summed(row, window, none, other, came)


def written(pair, pairs, row, block, out, sem):
    @pl.when(jnp.logical_and(pair >= 0, pair < pairs))
    def _():
        copy = pltpu.make_async_copy(block, out.at[0, pair, 0, pl.ds(row, block.shape[0])], sem)
        copy.start()
        copy.wait()


def write_kernel(step, cuts, pairs, *refs):
    blocks = refs[: len(cuts) - 1]
    out, sems = refs[-2:]
    pair = step - lax.axis_index("site")

    @pl.when(jnp.logical_and(pair >= 0, pair < pairs))
    def _():
        copies = []
        for k, block in enumerate(blocks):
            rows = pl.ds(cuts[k], cuts[k + 1] - cuts[k])
            copies.append(pltpu.make_async_copy(block, out.at[0, pair, 0, rows], sems.at[k]))
            copies[-1].start()
        for copy in copies:
            copy.wait()


def last_kernel(step, pairs, row, window, none, other, came, before, out, block, sem):
    del before
    block[...] = summed(row, window, none, other, came)
    written(step - lax.axis_index("site"), pairs, row, block, out, sem)


def call(kernel, in_specs, out_shape, flops=0, moved=0, limit=LIMIT, **more):
    return pl.pallas_call(
        kernel,
        out_shape=out_shape,
        in_specs=in_specs,
        compiler_params=pltpu.CompilerParams(vmem_limit_bytes=limit),
        cost_estimate=pl.CostEstimate(flops=flops, bytes_accessed=moved, transcendentals=0),
        **more,
    )


def per_device(env_in, bra, ket, sector_dims, flags):
    sections = lax.axis_size("site")
    sectors = lax.axis_size("sector")
    sector = lax.axis_index("sector")
    pairs = ket.shape[1]
    width = ket.shape[-1]
    steps = pairs + sections - 1
    cuts = bounds(width, PARTS)
    last_cuts = bounds(width, LAST_PARTS)
    even = sector % 2 == 0

    def at(j, q):
        return j * sectors + q

    everyone = [(j, q) for j in range(sections) for q in range(sectors)]
    swap_pairs = [(at(j, q), at(j, q ^ 1)) for j, q in everyone]

    def swapped(parts):
        return [lax.ppermute(part, AXES, swap_pairs) for part in parts]

    def working(step):
        return [step - p for p in range(pairs) if 0 <= step - p < sections]

    def up_pairs(step):
        work = working(step)
        if step + 1 == steps:
            return [(at(j, q), at(j, q + 2)) for j in work for q in range(sectors - 2)]
        half = sections // 2
        if sections != 4 or len({j % half for j in work}) != len(work) or 1 in work:
            return [(at(j, q), at(j, (q + 2) % sectors)) for j, q in everyone]
        found = []
        for j in range(half):
            up, back = (j + half, j) if j + half in work else (j, j + half)
            found += [(at(up, q), at(up, q + 2)) for q in range(sectors - 2)]
            found += [(at(back, q + 2), at(back, q)) for q in range(sectors - 2)]
            found += [(at(up, q), at(back, q)) for q in (sectors - 2, sectors - 1)]
            found += [(at(back, q), at(up, q)) for q in (0, 1)]
        return found

    def next_pairs(step):
        moves = [j for j in working(step) if j + 1 < sections]
        if sections == 4 and 1 not in moves:
            return [(at(j, q), at(j ^ 1, q)) for j in range(sections) for q in range(sectors)]
        return [(at(j, q), at((j + 1) % sections, q)) for j in range(sections) for q in range(sectors)]

    def block(rows, dtype=jnp.bfloat16):
        return jax.ShapeDtypeStruct((rows, width), dtype)

    def blocks_of(parts):
        return [block(end - start) for start, end in zip(parts, parts[1:])]

    def chunk(step, start, end, groups, held, before, dtype, parts=None):
        fresh = step < pairs
        operands = [flag_rows] + ([entering] if fresh else []) + held[start:end] + [ket, bra] + before
        return call(
            functools.partial(step_kernel, step, cuts[start], end - start, fresh, len(before) > 0, groups, parts),
            [VMEM] * len(operands),
            [block(width, dtype)] * len(groups) if parts is None else blocks_of(parts),
            4 * sum(len(states) for states in groups) * (cuts[end] - cuts[start]) * width**2,
            out_specs=[VMEM] * (len(groups) if parts is None else len(parts) - 1),
        )(*operands)

    flag_here = flags.reshape(flags.shape[1])
    whole = jax.ShapeDtypeStruct((1, pairs, 1, width, width), jnp.bfloat16)
    result = None
    held = None
    for step in range(steps):
        if step == 0:
            first, later = (1, 2), (3, 0)
            copies = 1 + 2 * len(first) + 2 * len(later)
            stack = lambda n: jax.ShapeDtypeStruct((n, width, width), jnp.bfloat16)
            *single, e, blocks, flag_rows = call(
                functools.partial(open_kernel, first, later, cuts),
                [pl.BlockSpec(memory_space=pltpu.HBM)] * 5,
                blocks_of(cuts)
                + [
                    block(width),
                    stack(2 * len(later)),
                    jax.ShapeDtypeStruct((ket.shape[2], 8, width), jnp.float32),
                ],
                4 * len(first) * width**3,
                limit=OPEN_LIMIT,
                scratch_shapes=[
                    pltpu.SMEM(sector_dims.shape, jnp.int32),
                    pltpu.SMEM(flag_here.shape, jnp.int32),
                    pltpu.VMEM((width, width), jnp.bfloat16),
                    pltpu.VMEM((len(first), width, width), jnp.bfloat16),
                    pltpu.VMEM((len(first), width, width), jnp.bfloat16),
                    pltpu.SemaphoreType.DMA((2,)),
                    pltpu.SemaphoreType.DMA((copies,)),
                ],
                out_specs=[VMEM] * (CHUNKS + 3),
            )(*[pltpu.with_memory_space_constraint(a, pltpu.HBM) for a in (sector_dims, flag_here, env_in, ket, bra)])
            other = swapped(single)
            double, none = call(
                functools.partial(follow_kernel, later),
                [VMEM] * 3,
                [block(width)] * 2,
                4 * len(later) * width**3,
                out_specs=[VMEM] * 2,
            )(flag_rows, e, blocks)
            window, entering = call(
                setup_kernel,
                [SMEM, VMEM, ANY],
                [
                    block(width),
                    jax.ShapeDtypeStruct((max(pairs - 1, 1), width, width), jnp.bfloat16),
                ],
                out_specs=[VMEM] * 2,
            )(sector_dims, env_in, double)
        else:
            total = []
            for start, end in zip(JOINED, JOINED[1:]):
                total = chunk(step, start, end, [(1, 2), (3,), (0,)], held, list(total), jnp.float32)
            total = list(total)
            parts = cuts if step + 1 < steps else last_cuts
            single = chunk(step, CHUNKS - 1, CHUNKS, [(1, 2)], held, total[:1], jnp.bfloat16, parts)
            other = swapped(single)
            double, none = chunk(step, CHUNKS - 1, CHUNKS, [(3,), (0,)], held, total[1:], jnp.bfloat16)
        fresh = []
        if step + 1 == steps:
            cuts = last_cuts
        for k in range(len(cuts) - 1):
            rows = slice(cuts[k], cuts[k + 1])
            part = jnp.where(even, other[k].astype(jnp.float32), 0.0)
            up = (double[rows].astype(jnp.float32) + part).astype(jnp.bfloat16)
            came = lax.ppermute(up, AXES, up_pairs(step))
            operands = (window, none, other[k], came)
            if step + 1 < steps:
                fresh.append(
                    call(
                        functools.partial(sum_kernel, cuts[k]),
                        [VMEM] * 4,
                        block(cuts[k + 1] - cuts[k]),
                        out_specs=VMEM,
                    )(*operands)
                )
            else:
                result = call(
                    functools.partial(last_kernel, step, pairs, cuts[k]),
                    [VMEM] * 4 + [ANY],
                    whole,
                    out_specs=ANY,
                    scratch_shapes=[pltpu.VMEM((cuts[k + 1] - cuts[k], width), jnp.bfloat16), pltpu.SemaphoreType.DMA],
                    input_output_aliases={4: 0},
                )(*operands, result)
        if step + 1 == steps:
            break
        held = [lax.ppermute(rows, AXES, next_pairs(step)) for rows in fresh]
        operands = fresh + ([] if result is None else [result])
        result = call(
            functools.partial(write_kernel, step, cuts, pairs),
            [VMEM] * CHUNKS + [ANY] * (len(operands) - CHUNKS),
            whole,
            out_specs=ANY,
            scratch_shapes=[pltpu.SemaphoreType.DMA((CHUNKS,))],
            input_output_aliases={} if result is None else {CHUNKS: 0},
        )(*operands)
    return result


def solution(mesh):
    in_specs = (
        P(None, "sector", None, None),
        P("site", None, "sector", None, None),
        P("site", None, None, "sector", None, None),
        P(),
        P("site", None, "sector"),
    )
    out_specs = P("site", None, "sector", None, None)
    return jax.shard_map(per_device, mesh=mesh, in_specs=in_specs, out_specs=out_specs, check_vma=False)
```

```python
import functools

import jax
import jax.numpy as jnp
from jax import lax
from jax.experimental import pallas as pl
from jax.experimental.pallas import tpu as pltpu
from jax.sharding import PartitionSpec as P

PARTS = (8, 8, 8, 8)
CHUNKS = len(PARTS)
JOINED = (0, 2, 3)
LAST_PARTS = (21, 11)
AXES = ("site", "sector")
LIMIT = 20 << 20
OPEN_LIMIT = 20 << 20
SMEM = pl.BlockSpec(memory_space=pltpu.SMEM)
VMEM = pl.BlockSpec(memory_space=pltpu.VMEM)
ANY = pl.BlockSpec(memory_space=pl.ANY)


def bounds(width, parts):
    tiles = width // 16
    ends = [sum(parts[:k]) * tiles // sum(parts) for k in range(len(parts) + 1)]
    return [16 * end for end in ends]


def across(a, b):
    return lax.dot_general(a, b, (((1,), (0,)), ((), ())), preferred_element_type=jnp.float32)


def down(a, b):
    return lax.dot_general(a, b, (((0,), (0,)), ((), ())), preferred_element_type=jnp.float32)


def inside(shape, row, used):
    rows = lax.broadcasted_iota(jnp.int32, shape, 0) + row
    lanes = lax.broadcasted_iota(jnp.int32, shape, 1)
    return jnp.logical_and(rows < used, lanes < used)


def pair_of(step, pairs):
    return jnp.clip(step - lax.axis_index("site"), 0, pairs - 1)


def cut(block, row, dims):
    used = dims[0, lax.axis_index("sector")]
    return jnp.where(inside(block.shape, row, used), block.astype(jnp.float32), 0.0).astype(jnp.bfloat16)


def product(e, ket_block, bra_rows, flag):
    moved = across(e, ket_block) * flag
    return down(bra_rows, moved.astype(jnp.bfloat16))


def group(states, e, row, ket, bra, flags, pair, total):
    rows = slice(row, row + e.shape[0])
    moved = [(across(e, ket[0, pair, s, 0]) * flags[s, :1]).astype(jnp.bfloat16) for s in states]
    blocks = [bra[0, s, 0, rows] for s in states]
    part = down(jnp.concatenate(blocks, axis=0), jnp.concatenate(moved, axis=0))
    return part if total is None else total + part


def parted(total, cuts, outs):
    for start, end, out in zip(cuts, cuts[1:], outs):
        out[...] = total[start:end].astype(out.dtype)


def open_kernel(first, later, cuts, dims_in, flags_in, env, ket, bra, *refs):
    outs, (e_out, block_out, flag_rows, dims, flags, env_buf, ket_buf, bra_buf, small_sems, sems) = refs[: len(cuts) - 1], refs[len(cuts) - 1 :]
    ket_out, bra_out = block_out.at[: len(later)], block_out.at[len(later) :]
    pair = pair_of(0, ket.shape[1])
    copies = [pltpu.make_async_copy(env.at[0, 0], env_buf, sems.at[0])]
    for states, kets, bras in ((first, ket_buf, bra_buf), (later, ket_out, bra_out)):
        for i, s in enumerate(states):
            copies.append(pltpu.make_async_copy(ket.at[0, pair, s, 0], kets.at[i], sems.at[len(copies)]))
            copies.append(pltpu.make_async_copy(bra.at[0, s, 0], bras.at[i], sems.at[len(copies)]))
    soon = 1 + 2 * len(first)
    small = [
        pltpu.make_async_copy(dims_in, dims, small_sems.at[0]),
        pltpu.make_async_copy(flags_in, flags, small_sems.at[1]),
    ]
    for copy in small:
        copy.start()
    for copy in copies[:soon]:
        copy.start()
    for copy in small:
        copy.wait()
    copies[0].wait()
    for copy in copies[soon:]:
        copy.start()
    e = cut(env_buf[...], 0, dims)
    e_out[...] = e
    for s in range(flag_rows.shape[0]):
        flag_rows[s] = jnp.zeros(flag_rows.shape[1:], jnp.float32) + flags[s].astype(jnp.float32)
    total = None
    for i, s in enumerate(first):
        copies[1 + 2 * i].wait()
        copies[2 + 2 * i].wait()
        part = product(e, ket_buf[i], bra_buf[i], flags[s].astype(jnp.float32))
        total = part if total is None else total + part
    parted(total, cuts, outs)
    for copy in copies[1 + 2 * len(first) :]:
        copy.wait()


def follow_kernel(later, flags, e, blocks, *outs):
    for i, (s, out) in enumerate(zip(later, outs)):
        out[...] = product(e[...], blocks[i], blocks[len(later) + i], flags[s, :1]).astype(jnp.bfloat16)


def setup_kernel(dims, env, after, window, entering):
    del after
    used = dims[lax.axis_index("site") + 1, lax.axis_index("sector")]
    window[...] = jnp.where(inside(window.shape, 0, used), 1.0, 0.0).astype(window.dtype)
    for p in range(entering.shape[0]):
        entering[p] = cut(env[p + 1, 0], 0, dims)


def step_kernel(step, row, count, fresh, added, groups, cuts, flags, *refs):
    refs = list(refs)
    entering = refs.pop(0) if fresh else None
    held, (ket, bra) = refs[:count], refs[count : count + 2]
    refs = refs[count + 2 :]
    before = refs[: len(groups)] if added else [None] * len(groups)
    outs = refs[len(groups) * added :]
    pair = pair_of(step, ket.shape[1])
    e = jnp.concatenate([rows[...] for rows in held], axis=0)
    if fresh:
        e = jnp.where(lax.axis_index("site") == 0, entering[step - 1, row : row + e.shape[0]], e)
    for states, start, out in zip(groups, before, outs):
        total = group(states, e, row, ket, bra, flags, pair, None if start is None else start[...])
        if cuts is None:
            out[...] = total.astype(out.dtype)
        else:
            parted(total, cuts, outs)


def summed(row, window, none, other, came):
    rows = slice(row, row + came.shape[0])
    sector = lax.axis_index("sector")
    total = none[rows].astype(jnp.float32)
    total = total + jnp.where(sector % 2 == 1, other[...].astype(jnp.float32), 0.0)
    total = total + jnp.where(sector >= 2, came[...].astype(jnp.float32), 0.0)
    return (total * window[rows].astype(jnp.float32)).astype(jnp.bfloat16)


def sum_kernel(row, window, none, other, came, out):
    out[...] = summed(row, window, none, other, came)


def written(pair, pairs, row, block, out, sem):
    @pl.when(jnp.logical_and(pair >= 0, pair < pairs))
    def _():
        copy = pltpu.make_async_copy(block, out.at[0, pair, 0, pl.ds(row, block.shape[0])], sem)
        copy.start()
        copy.wait()


def write_kernel(step, cuts, pairs, *refs):
    blocks = refs[: len(cuts) - 1]
    out, sems = refs[-2:]
    pair = step - lax.axis_index("site")

    @pl.when(jnp.logical_and(pair >= 0, pair < pairs))
    def _():
        copies = []
        for k, block in enumerate(blocks):
            rows = pl.ds(cuts[k], cuts[k + 1] - cuts[k])
            copies.append(pltpu.make_async_copy(block, out.at[0, pair, 0, rows], sems.at[k]))
            copies[-1].start()
        for copy in copies:
            copy.wait()


def last_kernel(step, pairs, row, window, none, other, came, before, out, block, sem):
    del before
    block[...] = summed(row, window, none, other, came)
    written(step - lax.axis_index("site"), pairs, row, block, out, sem)


def call(kernel, in_specs, out_shape, flops=0, moved=0, limit=LIMIT, **more):
    return pl.pallas_call(
        kernel,
        out_shape=out_shape,
        in_specs=in_specs,
        compiler_params=pltpu.CompilerParams(vmem_limit_bytes=limit),
        cost_estimate=pl.CostEstimate(flops=flops, bytes_accessed=moved, transcendentals=0),
        **more,
    )


def per_device(env_in, bra, ket, sector_dims, flags):
    sections = lax.axis_size("site")
    sectors = lax.axis_size("sector")
    sector = lax.axis_index("sector")
    pairs = ket.shape[1]
    width = ket.shape[-1]
    steps = pairs + sections - 1
    cuts = bounds(width, PARTS)
    last_cuts = bounds(width, LAST_PARTS)
    even = sector % 2 == 0

    def at(j, q):
        return j * sectors + q

    everyone = [(j, q) for j in range(sections) for q in range(sectors)]
    swap_pairs = [(at(j, q), at(j, q ^ 1)) for j, q in everyone]

    def swapped(parts):
        return [lax.ppermute(part, AXES, swap_pairs) for part in parts]

    def working(step):
        return [step - p for p in range(pairs) if 0 <= step - p < sections]

    def up_pairs(step):
        work = working(step)
        if step + 1 == steps:
            return [(at(j, q), at(j, q + 2)) for j in work for q in range(sectors - 2)]
        half = sections // 2
        if sections != 4 or len({j % half for j in work}) != len(work) or 1 in work:
            return [(at(j, q), at(j, (q + 2) % sectors)) for j, q in everyone]
        found = []
        for j in range(half):
            up, back = (j + half, j) if j + half in work else (j, j + half)
            found += [(at(up, q), at(up, q + 2)) for q in range(sectors - 2)]
            found += [(at(back, q + 2), at(back, q)) for q in range(sectors - 2)]
            found += [(at(up, q), at(back, q)) for q in (sectors - 2, sectors - 1)]
            found += [(at(back, q), at(up, q)) for q in (0, 1)]
        return found

    def next_pairs(step):
        moves = [j for j in working(step) if j + 1 < sections]
        if sections == 4 and 1 not in moves:
            return [(at(j, q), at(j ^ 1, q)) for j in range(sections) for q in range(sectors)]
        return [(at(j, q), at((j + 1) % sections, q)) for j in range(sections) for q in range(sectors)]

    def block(rows, dtype=jnp.bfloat16):
        return jax.ShapeDtypeStruct((rows, width), dtype)

    def blocks_of(parts):
        return [block(end - start) for start, end in zip(parts, parts[1:])]

    def chunk(step, start, end, groups, held, before, dtype, parts=None):
        fresh = step < pairs
        operands = [flag_rows] + ([entering] if fresh else []) + held[start:end] + [ket, bra] + before
        return call(
            functools.partial(step_kernel, step, cuts[start], end - start, fresh, len(before) > 0, groups, parts),
            [VMEM] * len(operands),
            [block(width, dtype)] * len(groups) if parts is None else blocks_of(parts),
            4 * sum(len(states) for states in groups) * (cuts[end] - cuts[start]) * width**2,
            out_specs=[VMEM] * (len(groups) if parts is None else len(parts) - 1),
        )(*operands)

    flag_here = flags.reshape(flags.shape[1])
    whole = jax.ShapeDtypeStruct((1, pairs, 1, width, width), jnp.bfloat16)
    result = None
    held = None
    for step in range(steps):
        if step == 0:
            first, later = (1, 2), (3, 0)
            copies = 1 + 2 * len(first) + 2 * len(later)
            stack = lambda n: jax.ShapeDtypeStruct((n, width, width), jnp.bfloat16)
            *single, e, blocks, flag_rows = call(
                functools.partial(open_kernel, first, later, cuts),
                [pl.BlockSpec(memory_space=pltpu.HBM)] * 5,
                blocks_of(cuts)
                + [
                    block(width),
                    stack(2 * len(later)),
                    jax.ShapeDtypeStruct((ket.shape[2], 8, width), jnp.float32),
                ],
                4 * len(first) * width**3,
                limit=OPEN_LIMIT,
                scratch_shapes=[
                    pltpu.SMEM(sector_dims.shape, jnp.int32),
                    pltpu.SMEM(flag_here.shape, jnp.int32),
                    pltpu.VMEM((width, width), jnp.bfloat16),
                    pltpu.VMEM((len(first), width, width), jnp.bfloat16),
                    pltpu.VMEM((len(first), width, width), jnp.bfloat16),
                    pltpu.SemaphoreType.DMA((2,)),
                    pltpu.SemaphoreType.DMA((copies,)),
                ],
                out_specs=[VMEM] * (CHUNKS + 3),
            )(*[pltpu.with_memory_space_constraint(a, pltpu.HBM) for a in (sector_dims, flag_here, env_in, ket, bra)])
            other = swapped(single)
            double, none = call(
                functools.partial(follow_kernel, later),
                [VMEM] * 3,
                [block(width)] * 2,
                4 * len(later) * width**3,
                out_specs=[VMEM] * 2,
            )(flag_rows, e, blocks)
            window, entering = call(
                setup_kernel,
                [SMEM, VMEM, ANY],
                [
                    block(width),
                    jax.ShapeDtypeStruct((max(pairs - 1, 1), width, width), jnp.bfloat16),
                ],
                out_specs=[VMEM] * 2,
            )(sector_dims, env_in, double)
        else:
            total = []
            for start, end in zip(JOINED, JOINED[1:]):
                total = chunk(step, start, end, [(1, 2), (3,), (0,)], held, list(total), jnp.float32)
            total = list(total)
            parts = [0, width] if step + 1 < steps else last_cuts
            single = chunk(step, CHUNKS - 1, CHUNKS, [(1, 2)], held, total[:1], jnp.bfloat16, parts)
            other = swapped(single)
            if step + 1 < steps:
                other = [other[0][cuts[k] : cuts[k + 1]] for k in range(CHUNKS)]
            double, none = chunk(step, CHUNKS - 1, CHUNKS, [(3,), (0,)], held, total[1:], jnp.bfloat16)
        fresh = []
        if step + 1 == steps:
            cuts = last_cuts
        for k in range(len(cuts) - 1):
            rows = slice(cuts[k], cuts[k + 1])
            part = jnp.where(even, other[k].astype(jnp.float32), 0.0)
            up = (double[rows].astype(jnp.float32) + part).astype(jnp.bfloat16)
            came = lax.ppermute(up, AXES, up_pairs(step))
            operands = (window, none, other[k], came)
            if step + 1 < steps:
                fresh.append(
                    call(
                        functools.partial(sum_kernel, cuts[k]),
                        [VMEM] * 4,
                        block(cuts[k + 1] - cuts[k]),
                        out_specs=VMEM,
                    )(*operands)
                )
            else:
                result = call(
                    functools.partial(last_kernel, step, pairs, cuts[k]),
                    [VMEM] * 4 + [ANY],
                    whole,
                    out_specs=ANY,
                    scratch_shapes=[pltpu.VMEM((cuts[k + 1] - cuts[k], width), jnp.bfloat16), pltpu.SemaphoreType.DMA],
                    input_output_aliases={4: 0},
                )(*operands, result)
        if step + 1 == steps:
            break
        held = [lax.ppermute(rows, AXES, next_pairs(step)) for rows in fresh]
        operands = fresh + ([] if result is None else [result])
        result = call(
            functools.partial(write_kernel, step, cuts, pairs),
            [VMEM] * CHUNKS + [ANY] * (len(operands) - CHUNKS),
            whole,
            out_specs=ANY,
            scratch_shapes=[pltpu.SemaphoreType.DMA((CHUNKS,))],
            input_output_aliases={} if result is None else {CHUNKS: 0},
        )(*operands)
    return result


def solution(mesh):
    in_specs = (
        P(None, "sector", None, None),
        P("site", None, "sector", None, None),
        P("site", None, None, "sector", None, None),
        P(),
        P("site", None, "sector"),
    )
    out_specs = P("site", None, "sector", None, None)
    return jax.shard_map(per_device, mesh=mesh, in_specs=in_specs, out_specs=out_specs, check_vma=False)
```

```python
import functools

import jax
import jax.numpy as jnp
from jax import lax
from jax.experimental import pallas as pl
from jax.experimental.pallas import tpu as pltpu
from jax.sharding import PartitionSpec as P

PARTS = (8, 8, 8, 8)
CHUNKS = len(PARTS)
JOINED = (0, 1, 3)
LAST_PARTS = (21, 11)
AXES = ("site", "sector")
LIMIT = 20 << 20
OPEN_LIMIT = 20 << 20
SMEM = pl.BlockSpec(memory_space=pltpu.SMEM)
VMEM = pl.BlockSpec(memory_space=pltpu.VMEM)
ANY = pl.BlockSpec(memory_space=pl.ANY)


def bounds(width, parts):
    tiles = width // 16
    ends = [sum(parts[:k]) * tiles // sum(parts) for k in range(len(parts) + 1)]
    return [16 * end for end in ends]


def across(a, b):
    return lax.dot_general(a, b, (((1,), (0,)), ((), ())), preferred_element_type=jnp.float32)


def down(a, b):
    return lax.dot_general(a, b, (((0,), (0,)), ((), ())), preferred_element_type=jnp.float32)


def inside(shape, row, used):
    rows = lax.broadcasted_iota(jnp.int32, shape, 0) + row
    lanes = lax.broadcasted_iota(jnp.int32, shape, 1)
    return jnp.logical_and(rows < used, lanes < used)


def pair_of(step, pairs):
    return jnp.clip(step - lax.axis_index("site"), 0, pairs - 1)


def cut(block, row, dims):
    used = dims[0, lax.axis_index("sector")]
    return jnp.where(inside(block.shape, row, used), block.astype(jnp.float32), 0.0).astype(jnp.bfloat16)


def product(e, ket_block, bra_rows, flag):
    moved = across(e, ket_block) * flag
    return down(bra_rows, moved.astype(jnp.bfloat16))


def group(states, e, row, ket, bra, flags, pair, total):
    rows = slice(row, row + e.shape[0])
    moved = [(across(e, ket[0, pair, s, 0]) * flags[s, :1]).astype(jnp.bfloat16) for s in states]
    blocks = [bra[0, s, 0, rows] for s in states]
    part = down(jnp.concatenate(blocks, axis=0), jnp.concatenate(moved, axis=0))
    return part if total is None else total + part


def parted(total, cuts, outs):
    for start, end, out in zip(cuts, cuts[1:], outs):
        out[...] = total[start:end].astype(out.dtype)


def open_kernel(first, later, cuts, dims_in, flags_in, env, ket, bra, *refs):
    outs, (e_out, block_out, flag_rows, dims, flags, env_buf, ket_buf, bra_buf, small_sems, sems) = refs[: len(cuts) - 1], refs[len(cuts) - 1 :]
    ket_out, bra_out = block_out.at[: len(later)], block_out.at[len(later) :]
    pair = pair_of(0, ket.shape[1])
    copies = [pltpu.make_async_copy(env.at[0, 0], env_buf, sems.at[0])]
    for states, kets, bras in ((first, ket_buf, bra_buf), (later, ket_out, bra_out)):
        for i, s in enumerate(states):
            copies.append(pltpu.make_async_copy(ket.at[0, pair, s, 0], kets.at[i], sems.at[len(copies)]))
            copies.append(pltpu.make_async_copy(bra.at[0, s, 0], bras.at[i], sems.at[len(copies)]))
    soon = 1 + 2 * len(first)
    small = [
        pltpu.make_async_copy(dims_in, dims, small_sems.at[0]),
        pltpu.make_async_copy(flags_in, flags, small_sems.at[1]),
    ]
    for copy in small:
        copy.start()
    for copy in copies[:soon]:
        copy.start()
    for copy in small:
        copy.wait()
    copies[0].wait()
    for copy in copies[soon:]:
        copy.start()
    e = cut(env_buf[...], 0, dims)
    e_out[...] = e
    for s in range(flag_rows.shape[0]):
        flag_rows[s] = jnp.zeros(flag_rows.shape[1:], jnp.float32) + flags[s].astype(jnp.float32)
    total = None
    for i, s in enumerate(first):
        copies[1 + 2 * i].wait()
        copies[2 + 2 * i].wait()
        part = product(e, ket_buf[i], bra_buf[i], flags[s].astype(jnp.float32))
        total = part if total is None else total + part
    parted(total, cuts, outs)
    for copy in copies[1 + 2 * len(first) :]:
        copy.wait()


def follow_kernel(later, flags, e, blocks, *outs):
    for i, (s, out) in enumerate(zip(later, outs)):
        out[...] = product(e[...], blocks[i], blocks[len(later) + i], flags[s, :1]).astype(jnp.bfloat16)


def setup_kernel(dims, env, after, window, entering):
    del after
    used = dims[lax.axis_index("site") + 1, lax.axis_index("sector")]
    window[...] = jnp.where(inside(window.shape, 0, used), 1.0, 0.0).astype(window.dtype)
    for p in range(entering.shape[0]):
        entering[p] = cut(env[p + 1, 0], 0, dims)


def step_kernel(step, row, count, fresh, added, groups, cuts, flags, *refs):
    refs = list(refs)
    entering = refs.pop(0) if fresh else None
    held, (ket, bra) = refs[:count], refs[count : count + 2]
    refs = refs[count + 2 :]
    before = refs[: len(groups)] if added else [None] * len(groups)
    outs = refs[len(groups) * added :]
    pair = pair_of(step, ket.shape[1])
    e = jnp.concatenate([rows[...] for rows in held], axis=0)
    if fresh:
        e = jnp.where(lax.axis_index("site") == 0, entering[step - 1, row : row + e.shape[0]], e)
    for states, start, out in zip(groups, before, outs):
        total = group(states, e, row, ket, bra, flags, pair, None if start is None else start[...])
        if cuts is None:
            out[...] = total.astype(out.dtype)
        else:
            parted(total, cuts, outs)


def summed(row, window, none, other, came):
    rows = slice(row, row + came.shape[0])
    sector = lax.axis_index("sector")
    total = none[rows].astype(jnp.float32)
    total = total + jnp.where(sector % 2 == 1, other[...].astype(jnp.float32), 0.0)
    total = total + jnp.where(sector >= 2, came[...].astype(jnp.float32), 0.0)
    return (total * window[rows].astype(jnp.float32)).astype(jnp.bfloat16)


def sum_kernel(row, window, none, other, came, out):
    out[...] = summed(row, window, none, other, came)


def written(pair, pairs, row, block, out, sem):
    @pl.when(jnp.logical_and(pair >= 0, pair < pairs))
    def _():
        copy = pltpu.make_async_copy(block, out.at[0, pair, 0, pl.ds(row, block.shape[0])], sem)
        copy.start()
        copy.wait()


def write_kernel(step, cuts, pairs, *refs):
    blocks = refs[: len(cuts) - 1]
    out, sems = refs[-2:]
    pair = step - lax.axis_index("site")

    @pl.when(jnp.logical_and(pair >= 0, pair < pairs))
    def _():
        copies = []
        for k, block in enumerate(blocks):
            rows = pl.ds(cuts[k], cuts[k + 1] - cuts[k])
            copies.append(pltpu.make_async_copy(block, out.at[0, pair, 0, rows], sems.at[k]))
            copies[-1].start()
        for copy in copies:
            copy.wait()


def last_kernel(step, pairs, row, window, none, other, came, before, out, block, sem):
    del before
    block[...] = summed(row, window, none, other, came)
    written(step - lax.axis_index("site"), pairs, row, block, out, sem)


def call(kernel, in_specs, out_shape, flops=0, moved=0, limit=LIMIT, **more):
    return pl.pallas_call(
        kernel,
        out_shape=out_shape,
        in_specs=in_specs,
        compiler_params=pltpu.CompilerParams(vmem_limit_bytes=limit),
        cost_estimate=pl.CostEstimate(flops=flops, bytes_accessed=moved, transcendentals=0),
        **more,
    )


def per_device(env_in, bra, ket, sector_dims, flags):
    sections = lax.axis_size("site")
    sectors = lax.axis_size("sector")
    sector = lax.axis_index("sector")
    pairs = ket.shape[1]
    width = ket.shape[-1]
    steps = pairs + sections - 1
    cuts = bounds(width, PARTS)
    last_cuts = bounds(width, LAST_PARTS)
    even = sector % 2 == 0

    def at(j, q):
        return j * sectors + q

    everyone = [(j, q) for j in range(sections) for q in range(sectors)]
    swap_pairs = [(at(j, q), at(j, q ^ 1)) for j, q in everyone]

    def swapped(parts):
        return [lax.ppermute(part, AXES, swap_pairs) for part in parts]

    def working(step):
        return [step - p for p in range(pairs) if 0 <= step - p < sections]

    def up_pairs(step):
        work = working(step)
        if step + 1 == steps:
            return [(at(j, q), at(j, q + 2)) for j in work for q in range(sectors - 2)]
        half = sections // 2
        if sections != 4 or len({j % half for j in work}) != len(work) or 1 in work:
            return [(at(j, q), at(j, (q + 2) % sectors)) for j, q in everyone]
        found = []
        for j in range(half):
            up, back = (j + half, j) if j + half in work else (j, j + half)
            found += [(at(up, q), at(up, q + 2)) for q in range(sectors - 2)]
            found += [(at(back, q + 2), at(back, q)) for q in range(sectors - 2)]
            found += [(at(up, q), at(back, q)) for q in (sectors - 2, sectors - 1)]
            found += [(at(back, q), at(up, q)) for q in (0, 1)]
        return found

    def next_pairs(step):
        moves = [j for j in working(step) if j + 1 < sections]
        if sections == 4 and 1 not in moves:
            return [(at(j, q), at(j ^ 1, q)) for j in range(sections) for q in range(sectors)]
        return [(at(j, q), at((j + 1) % sections, q)) for j in range(sections) for q in range(sectors)]

    def block(rows, dtype=jnp.bfloat16):
        return jax.ShapeDtypeStruct((rows, width), dtype)

    def blocks_of(parts):
        return [block(end - start) for start, end in zip(parts, parts[1:])]

    def chunk(step, start, end, groups, held, before, dtype, parts=None):
        fresh = step < pairs
        operands = [flag_rows] + ([entering] if fresh else []) + held[start:end] + [ket, bra] + before
        return call(
            functools.partial(step_kernel, step, cuts[start], end - start, fresh, len(before) > 0, groups, parts),
            [VMEM] * len(operands),
            [block(width, dtype)] * len(groups) if parts is None else blocks_of(parts),
            4 * sum(len(states) for states in groups) * (cuts[end] - cuts[start]) * width**2,
            out_specs=[VMEM] * (len(groups) if parts is None else len(parts) - 1),
        )(*operands)

    flag_here = flags.reshape(flags.shape[1])
    whole = jax.ShapeDtypeStruct((1, pairs, 1, width, width), jnp.bfloat16)
    result = None
    held = None
    for step in range(steps):
        if step == 0:
            first, later = (1, 2), (3, 0)
            copies = 1 + 2 * len(first) + 2 * len(later)
            stack = lambda n: jax.ShapeDtypeStruct((n, width, width), jnp.bfloat16)
            *single, e, blocks, flag_rows = call(
                functools.partial(open_kernel, first, later, cuts),
                [pl.BlockSpec(memory_space=pltpu.HBM)] * 5,
                blocks_of(cuts)
                + [
                    block(width),
                    stack(2 * len(later)),
                    jax.ShapeDtypeStruct((ket.shape[2], 8, width), jnp.float32),
                ],
                4 * len(first) * width**3,
                limit=OPEN_LIMIT,
                scratch_shapes=[
                    pltpu.SMEM(sector_dims.shape, jnp.int32),
                    pltpu.SMEM(flag_here.shape, jnp.int32),
                    pltpu.VMEM((width, width), jnp.bfloat16),
                    pltpu.VMEM((len(first), width, width), jnp.bfloat16),
                    pltpu.VMEM((len(first), width, width), jnp.bfloat16),
                    pltpu.SemaphoreType.DMA((2,)),
                    pltpu.SemaphoreType.DMA((copies,)),
                ],
                out_specs=[VMEM] * (CHUNKS + 3),
            )(*[pltpu.with_memory_space_constraint(a, pltpu.HBM) for a in (sector_dims, flag_here, env_in, ket, bra)])
            other = swapped(single)
            double, none = call(
                functools.partial(follow_kernel, later),
                [VMEM] * 3,
                [block(width)] * 2,
                4 * len(later) * width**3,
                out_specs=[VMEM] * 2,
            )(flag_rows, e, blocks)
            window, entering = call(
                setup_kernel,
                [SMEM, VMEM, ANY],
                [
                    block(width),
                    jax.ShapeDtypeStruct((max(pairs - 1, 1), width, width), jnp.bfloat16),
                ],
                out_specs=[VMEM] * 2,
            )(sector_dims, env_in, double)
        else:
            total = []
            for start, end in zip(JOINED, JOINED[1:]):
                total = chunk(step, start, end, [(1, 2), (3,), (0,)], held, list(total), jnp.float32)
            total = list(total)
            parts = cuts if step + 1 < steps else last_cuts
            single = chunk(step, CHUNKS - 1, CHUNKS, [(1, 2)], held, total[:1], jnp.bfloat16, parts)
            other = swapped(single)
            double, none = chunk(step, CHUNKS - 1, CHUNKS, [(3,), (0,)], held, total[1:], jnp.bfloat16)
        fresh = []
        if step + 1 == steps:
            cuts = last_cuts
        for k in range(len(cuts) - 1):
            rows = slice(cuts[k], cuts[k + 1])
            part = jnp.where(even, other[k].astype(jnp.float32), 0.0)
            up = (double[rows].astype(jnp.float32) + part).astype(jnp.bfloat16)
            came = lax.ppermute(up, AXES, up_pairs(step))
            operands = (window, none, other[k], came)
            if step + 1 < steps:
                fresh.append(
                    call(
                        functools.partial(sum_kernel, cuts[k]),
                        [VMEM] * 4,
                        block(cuts[k + 1] - cuts[k]),
                        out_specs=VMEM,
                    )(*operands)
                )
            else:
                result = call(
                    functools.partial(last_kernel, step, pairs, cuts[k]),
                    [VMEM] * 4 + [ANY],
                    whole,
                    out_specs=ANY,
                    scratch_shapes=[pltpu.VMEM((cuts[k + 1] - cuts[k], width), jnp.bfloat16), pltpu.SemaphoreType.DMA],
                    input_output_aliases={4: 0},
                )(*operands, result)
        if step + 1 == steps:
            break
        held = [lax.ppermute(rows, AXES, next_pairs(step)) for rows in fresh]
        operands = fresh + ([] if result is None else [result])
        result = call(
            functools.partial(write_kernel, step, cuts, pairs),
            [VMEM] * CHUNKS + [ANY] * (len(operands) - CHUNKS),
            whole,
            out_specs=ANY,
            scratch_shapes=[pltpu.SemaphoreType.DMA((CHUNKS,))],
            input_output_aliases={} if result is None else {CHUNKS: 0},
        )(*operands)
    return result


def solution(mesh):
    in_specs = (
        P(None, "sector", None, None),
        P("site", None, "sector", None, None),
        P("site", None, None, "sector", None, None),
        P(),
        P("site", None, "sector"),
    )
    out_specs = P("site", None, "sector", None, None)
    return jax.shard_map(per_device, mesh=mesh, in_specs=in_specs, out_specs=out_specs, check_vma=False)
```
